32 devices in a mesh: node: 8 (over z, x), rep: 4 (over y, core).
Axes of the slice: x: 2, y: 2, z: 4, core: 2. Of those that a mesh axis runs over, the one named last changes fastest.
Arguments:
- features: bfloat16 [8192, 512], P(('node', 'rep')), may hold values from -6 to 6
- weight: bfloat16 [512, 512], replicated, may hold values from -0.25 to 0.25
- cotangent: bfloat16 [8192, 512], P(('node', 'rep')), may hold values from -6 to 6
- tile_values: bfloat16 [8192, 128, 128], P(('node', 'rep')), may hold values from -0.125 to 0.125
- tile_row: int32 [8192], P(('node', 'rep')), may hold values from 0 to 7
- tile_col: int32 [8192], P(('node', 'rep')), may hold values from 0 to 15
- tile_count: int32 [32], P(('node', 'rep')), may hold values from 64 to 256, as said below
Outputs:
- activation: bfloat16 [8192, 512], P(('node', 'rep'))
- weight_grad: float32 [512, 512], replicated
- feature_grad: bfloat16 [8192, 512], P(('node', 'rep'))
The draws below stay inside these ranges and needn't reach their ends.
Inputs may be any that keep to these rules, and one draw needn't show every extreme that they name: `tile_count`: slots of a device below its count hold tiles, the others are ignored; some device uses all 256 slots.
All inputs are finite; a program needn't handle non-finite values.
Results may differ from the reference program's by a relative error of at most 0.023.
Values may be sent and summed in bfloat16 or wider, within the bound.
A program may use at most 128 MiB of HBM per device.

```python
import math
import jax
import jax.numpy as jnp
from jax import lax

F = 512
TB = 128
ROWS_DEV = 1024
CAP = 256
NODES = 8192
BLOCKS_DEV = 8
SUB_BLOCKS = 2
TILES = 8192
N_NODE = 8
N_REP = 4
DEVICES = 32


def draw_tile_count(key, part):
    counts_drawn = jax.random.randint(key, (DEVICES,), CAP // 4, 3 * CAP // 4 + 1, dtype=jnp.int32)
    busiest = jax.random.randint(jax.random.fold_in(key, 7), (), 0, DEVICES, dtype=jnp.int32)
    return jnp.where(jnp.arange(DEVICES, dtype=jnp.int32) == busiest, CAP, counts_drawn).astype(jnp.int32)


def set_ends(array, key, least, largest):
    extent = array.shape
    spot = [jax.random.randint(jax.random.fold_in(key, axis), (), 0, extent[axis]) for axis in range(len(extent))]
    array = array.at[tuple(spot)].set(least)
    longest = extent.index(max(extent))
    spot[longest] = (spot[longest] + 1) % extent[longest]
    return array.at[tuple(spot)].set(largest)


def level_of(key, extent, pieces, low, high):
    def one(dim, blocks):
        draws = jax.random.uniform(jax.random.fold_in(jax.random.fold_in(key, 6), dim), (blocks,), jnp.float32, low / len(pieces), high / len(pieces))
        return jnp.repeat(jnp.exp(draws), extent[dim] // blocks).reshape((-1,) + (1,) * (len(extent) - dim - 1))

    factor_of = one(*pieces[0])
    for cut in pieces[1:]:
        factor_of = factor_of * one(*cut)
    return factor_of


def bell_draw(key, shape, width, limit, cuts=(), held_as=jnp.bfloat16):
    loudness = level_of(key, shape, cuts, -0.22, 0.18) if cuts else 1.0
    drawn = jax.random.normal(key, shape, jnp.float32) * width * loudness
    return jnp.minimum(jnp.maximum(drawn, -limit), limit).astype(held_as)


def setup_inputs(seed: int = 0) -> dict:
    keys = jax.random.split(jax.random.key(seed), 8)
    return {
        "features": bell_draw(keys[0], (NODES, F), 1.0, 6.0, ((0, 32),)),
        "weight": bell_draw(keys[1], (F, F), F ** -0.5, 0.25),
        "cotangent": bell_draw(keys[2], (NODES, F), 1.0, 6.0, ((0, 32),)),
        "tile_values": bell_draw(keys[3], (TILES, TB, TB), (CAP * TB * TB // (2 * ROWS_DEV)) ** -0.5, 0.125, ((0, 32),)),
        "tile_row": set_ends(jax.random.randint(keys[4], (TILES,), 0, BLOCKS_DEV), jax.random.fold_in(keys[4], 1), 0, BLOCKS_DEV - 1).astype(jnp.int32),
        "tile_col": set_ends(jax.random.randint(keys[5], (TILES,), 0, N_NODE * SUB_BLOCKS), jax.random.fold_in(keys[5], 1), 0, (N_NODE * SUB_BLOCKS) - 1).astype(jnp.int32),
        "tile_count": draw_tile_count(jax.random.fold_in(keys[7], 71), 0),
    }


def smooth_gate(values):
    return jax.nn.gelu(values, approximate=True)

def tile_places(tile_row, tile_col):
    slot_index = jnp.arange(TILES, dtype=jnp.int32)
    device_index = slot_index // CAP
    node_index = device_index // N_REP
    rep_index = device_index % N_REP
    row_blocks = node_index * BLOCKS_DEV + tile_row
    col_blocks = tile_col // SUB_BLOCKS * BLOCKS_DEV + rep_index * SUB_BLOCKS + tile_col % SUB_BLOCKS
    return (row_blocks.astype(jnp.int32), col_blocks.astype(jnp.int32))

def reference(features, weight, cotangent, tile_values, tile_row, tile_col, tile_count):
    row_blocks, col_blocks = tile_places(tile_row, tile_col)
    slot_index = jnp.arange(TILES, dtype=jnp.int32)
    slot_live = (slot_index % CAP < jnp.repeat(tile_count, CAP)).astype(jnp.float32)
    per_device = (tile_values.reshape(DEVICES, CAP, TB, TB), row_blocks.reshape(DEVICES, CAP), col_blocks.reshape(DEVICES, CAP), slot_live.reshape(DEVICES, CAP))
    source_blocks = features.reshape(NODES // TB, TB, F)

    def forward_device(totals, packed):
        values, rows_here, cols_here, slot_mask = packed
        product = jnp.einsum('tij,tjf->tif', values.astype(jnp.float32), source_blocks[cols_here].astype(jnp.float32), precision=lax.Precision.HIGHEST)
        return (totals.at[rows_here].add(product * slot_mask[:, None, None]), None)
    sums = lax.scan(forward_device, jnp.zeros((NODES // TB, TB, F), jnp.float32), per_device)[0]
    aggregate = sums.reshape(NODES, F).astype(jnp.bfloat16)
    pre = jnp.dot(aggregate, weight, preferred_element_type=jnp.float32)
    activated, pullback = jax.vjp(smooth_gate, pre)
    pre_grad = pullback(cotangent.astype(jnp.float32))[0].astype(jnp.bfloat16)
    weight_grad = jnp.dot(aggregate.T, pre_grad, preferred_element_type=jnp.float32) * (1.0 / math.sqrt(NODES))
    row_grad = jnp.dot(pre_grad, weight.T, preferred_element_type=jnp.float32).astype(jnp.bfloat16)
    grad_blocks = row_grad.reshape(NODES // TB, TB, F)

    def backward_device(totals, packed):
        values, rows_here, cols_here, slot_mask = packed
        product = jnp.einsum('tji,tjf->tif', values.astype(jnp.float32), grad_blocks[rows_here].astype(jnp.float32), precision=lax.Precision.HIGHEST)
        return (totals.at[cols_here].add(product * slot_mask[:, None, None]), None)
    back_sums = lax.scan(backward_device, jnp.zeros((NODES // TB, TB, F), jnp.float32), per_device)[0]
    feature_grad = back_sums.reshape(NODES, F).astype(jnp.bfloat16)
    return (activated.astype(jnp.bfloat16), weight_grad, feature_grad)
```

```python
import functools
import math

import jax
import jax.numpy as jnp
from jax import lax
from jax.experimental import pallas as pl
from jax.experimental.pallas import tpu as pltpu
from jax.sharding import PartitionSpec as P

TB = 128
MESH = pl.DeviceIdType.MESH
BF = jnp.bfloat16
F32 = jnp.float32


def mm(a, b):
    return jnp.dot(a, b, preferred_element_type=F32)


def layer_kernel(
    cfg, key_ref, last_ref, x_ref, w_ref, c_ref, tiles_hbm,
    act_ref, wsum_ref, fg_ref,
    tiles, stage, dense, dense_t, X, part, psend, precv, agg, pre, pg, wt,
    rg, rsb, rrb, tbuf, aggt, wterm, wsend, wa, wb, wbs, wq, wc, wfull,
    tile_sem, gs, gr, ps, pr, as_, ar, rs, rr,
    was, war, wbss, wbr, wcs, wcr, wds, wdr, wes, wer, wfs, wfr,
):
    N, R, G, Q, D, T, cap, blocks, subs, has_t = cfg
    h = N // 2
    rows, F = x_ref.shape
    gw = F // G
    qr = rows // Q
    i = lax.axis_index("node")
    j = lax.axis_index("rep")
    z, x = lax.div(i, 2), lax.rem(i, 2)
    pos = z + x * (N - 1 - 2 * z)

    def node_at(k):
        p = lax.rem(pos + (k + N), N)
        xx = lax.div(p, N // 2)
        return 2 * (p + xx * (N - 1 - 2 * p)) + xx

    right, left = node_at(1), node_at(-1)
    ring_to = (right, left)
    sent = []

    def rcopy(src, dst, ssem, rsem, dev):
        return pltpu.make_async_remote_copy(
            src_ref=src, dst_ref=dst, send_sem=ssem, recv_sem=rsem,
            device_id=dev, device_id_type=MESH,
        )

    def send(src, dst, ssem, rsem, dev):
        c = rcopy(src, dst, ssem, rsem, dev)
        c.start()
        sent.append(c)

    def arrived(dst, ssem, rsem):
        rcopy(dst, dst, ssem, rsem, (i, j)).wait_recv()

    def half(d):
        return range(d * Q // 2, (d + 1) * Q // 2)

    def xat(o, q):
        return pl.ds(pl.multiple_of(o * rows + q * qr, qr), qr)

    per = cap // T
    tile_copies = [
        pltpu.make_async_copy(
            tiles_hbm.at[pl.ds(k * per, per)], tiles.at[pl.ds(k * per, per)], tile_sem.at[k]
        )
        for k in range(T)
    ]
    for c in tile_copies:
        c.start()

    barrier = pltpu.get_barrier_semaphore()
    for k in range(1, N):
        pl.semaphore_signal(barrier, inc=1, device_id=(lax.rem(i + k, N), j), device_id_type=MESH)
    for k in range(1, R):
        pl.semaphore_signal(barrier, inc=1, device_id=(i, lax.rem(j + k, R)), device_id_type=MESH)
    for g in range(G):
        X[g, pl.ds(pl.multiple_of(i * rows, rows), rows), :] = x_ref[:, g * gw:(g + 1) * gw]
    pl.semaphore_wait(barrier, N - 1 + R - 1)

    def gather_send(g, s, q, d):
        o = node_at(-s if d == 0 else s)
        at = xat(o, q)
        src = x_ref.at[pl.ds(q * qr, qr), pl.ds(g * gw, gw)] if s == 0 else X.at[g, at, :]
        send(src, X.at[g, at, :], gs.at[g, s, q, d], gr.at[g, s, q, d], (ring_to[d], j))

    def gather_start(g):
        for q in range(Q):
            for d in range(2):
                gather_send(g, 0, q, d)

    def gather_event(g, s, q):
        for d in range(2):
            if s == h - 1 and q not in half(d):
                continue
            o = node_at(-(s + 1) if d == 0 else s + 1)
            arrived(X.at[g, xat(o, q), :], gs.at[g, s, q, d], gr.at[g, s, q, d])
            if s + 1 < h and (s + 1 < h - 1 or q in half(d)):
                gather_send(g, s + 1, q, d)
        if s == max(h - 2, 0) and q == Q - 1 and g + 1 < G:
            gather_start(g + 1)

    events = [(g, s, q) for g in range(G) for s in range(h) for q in range(Q)]
    events.reverse()

    def event(count=1):
        for _ in range(count):
            if events:
                gather_event(*events.pop())

    gather_start(0)

    wt[...] = w_ref[...].T
    for c in tile_copies:
        c.wait()
    stage[cap] = jnp.zeros((TB, TB), BF)

    def slot_step(p, carry):
        acc, prev = carry
        key = key_ref[p]
        slot = lax.rem(key, cap)
        place = lax.div(key, cap)
        keep = jnp.where(place == prev, 1.0, 0.0).astype(F32)
        acc = acc * keep + tiles[slot].astype(F32)
        stage[p] = acc.astype(BF)
        return acc, place

    npieces = max(1, 3 * Q)
    carry = (jnp.zeros((TB, TB), F32), jnp.int32(-1))
    bounds = [cap * k // npieces for k in range(npieces + 1)]
    for k in range(npieces):
        carry = lax.fori_loop(bounds[k], bounds[k + 1], slot_step, carry)
        if k >= 3 and len(events) > (G - 1) * h * Q + Q:
            event()

    def place_step(o, carry):
        for r in range(blocks):
            for s in range(subs):
                tile = stage[last_ref[(o * blocks + r) * subs + s]]
                at = pl.ds(pl.multiple_of((o * subs + s) * TB, TB), TB)
                dense[r * TB:(r + 1) * TB, at] = tile
                if has_t:
                    dense_t[at, r * TB:(r + 1) * TB] = tile.T
        return carry

    for k in range(4):
        lax.fori_loop(N * k // 4, N * (k + 1) // 4, place_step, 0)
        if len(events) > (G - 1) * h * Q:
            event()
    while len(events) > (G - 1) * h * Q:
        event()

    def part_send(g, k):
        jj = lax.rem(j + k, R)
        psend[g, k - 1] = part[g, jj].astype(BF)
        send(psend.at[g, k - 1], precv.at[g, k - 1], ps.at[g, k - 1], pr.at[g, k - 1], (i, jj))

    def agg_group(g):
        total = part[g, j]
        for k in range(1, R):
            arrived(precv.at[g, k - 1], ps.at[g, k - 1], pr.at[g, k - 1])
            total += precv[g, k - 1].astype(F32)
        agg[:, g * gw:(g + 1) * gw] = total.astype(BF)

    def full_part(g, jj):
        at = pl.ds(pl.multiple_of(jj * rows, rows), rows)
        part[g, jj] = mm(dense[at, :], X[g])

    def block_part(g, offsets, first):
        def one(m, carry):
            at = pl.ds(pl.multiple_of(m * rows, rows), rows)
            total = None if first else part[g, m]
            for k in offsets:
                col = pl.ds(pl.multiple_of(node_at(k) * rows, rows), rows)
                t = mm(dense[at, col], X[g, col, :])
                total = t if total is None else total + t
            part[g, m] = total
            return carry

        lax.fori_loop(0, R, one, 0)

    def own_pre(g):
        t = mm(agg[:, g * gw:(g + 1) * gw], w_ref[g * gw:(g + 1) * gw, :])
        pre[...] = t if g == 0 else pre[...] + t

    for g in range(G):
        if g < G - 1:
            for k in range(1, R):
                full_part(g, lax.rem(j + k, R))
                part_send(g, k)
                event()
            full_part(g, j)
            left_over = (G - 2 - g) * h * Q
            agg_group(g)
            own_pre(g)
            while len(events) > left_over + h * Q - Q:
                event()
        else:
            block_part(g, [0], True)
            for s in range(h):
                while len(events) > (h - 1 - s) * Q:
                    event()
                block_part(g, [-(s + 1), s + 1] if s < h - 1 else [h], False)
            for k in range(1, R):
                part_send(g, k)
            agg_group(g)
            own_pre(g)

    root = math.sqrt(2.0 / math.pi)
    step = 32 if rows % 32 == 0 else rows

    def act_step(b, carry):
        at = pl.ds(pl.multiple_of(b * step, step), step)
        v = pre[at, :]
        v2 = v * v
        t = jnp.tanh(root * (v + 0.044715 * (v2 * v)))
        half_up = 0.5 * (1.0 + t)
        act_ref[at, :] = (v * half_up).astype(BF)
        slope = half_up + (0.5 * v) * (1.0 - t * t) * (root * (1.0 + (3 * 0.044715) * v2))
        pg[at, :] = (c_ref[at, :].astype(F32) * slope).astype(BF)
        return carry

    lax.fori_loop(0, rows // step, act_step, 0)

    for g in range(G):
        rg[g, j] = mm(pg[...], wt[:, g * gw:(g + 1) * gw]).astype(BF)
        for k in range(1, R):
            send(rg.at[g, j], rg.at[g, j], as_.at[g, k - 1], ar.at[g, k - 1], (i, lax.rem(j + k, R)))

    wr = F // R
    mine, par = lax.div(j, 2), lax.rem(j, 2)
    partner = (i, j + 1 - 2 * par)
    pa = min(N, wr // 16)
    pb = N // pa
    ph, pw = wr // pa, F // pb
    M = R // 2

    def weight_terms():
        aggt[...] = agg[...].T

        def one(k, carry):
            at = pl.ds(pl.multiple_of(k * wr, wr), wr)
            t = mm(aggt[at, :], pg[...])
            wterm[k] = t
            wsend[k] = t.astype(BF)
            return carry

        lax.fori_loop(0, R, one, 0)
        for m in range(M):
            send(wsend.at[2 * m + 1 - par], wa.at[m], was.at[m], war.at[m], partner)

    def weight_chip():
        for m in range(M):
            arrived(wa.at[m], was.at[m], war.at[m])
            wterm[2 * m + par] = wterm[2 * m + par] + wa[m].astype(F32)
        for k in range(1, M):
            to = lax.rem(mine + k, M)
            wbs[k - 1] = wterm[2 * to + par].astype(BF)
            send(wbs.at[k - 1], wb.at[k - 1], wbss.at[k - 1], wbr.at[k - 1], (i, 2 * to + par))

    def piece(n):
        return (
            pl.ds(pl.multiple_of(lax.div(n, pb) * ph, ph), ph),
            pl.ds(pl.multiple_of(lax.rem(n, pb) * pw, pw), pw),
        )

    def weight_rep():
        total = wterm[j]
        for k in range(1, M):
            arrived(wb.at[k - 1], wbss.at[k - 1], wbr.at[k - 1])
            total += wb[k - 1].astype(F32)
        wq[...] = total.astype(BF)
        for k in range(1, N):
            n = lax.rem(i + k, N)
            send(wq.at[piece(n)], wc.at[k - 1], wcs.at[k - 1], wcr.at[k - 1], (n, j))

    def weight_node():
        at = piece(i)
        total = wq[at].astype(F32)
        for k in range(1, N):
            arrived(wc.at[k - 1], wcs.at[k - 1], wcr.at[k - 1])
            total += wc[k - 1].astype(F32)
        wfull[(j,) + at] = total.astype(BF)
        for k in range(1, N):
            spot = wfull.at[(j,) + at]
            send(spot, spot, wds.at[k - 1], wdr.at[k - 1], (lax.rem(i + k, N), j))

    def weight_spread():
        for k in range(1, N):
            spot = wfull.at[(j,) + piece(lax.rem(i - k + N, N))]
            arrived(spot, wds.at[k - 1], wdr.at[k - 1])
        quarter = wfull.at[j]
        for k in range(1, M):
            to = 2 * lax.rem(mine + k, M) + par
            send(quarter, quarter, wes.at[k], wer.at[k], (i, to))
        send(quarter, quarter, wes.at[0], wer.at[0], partner)

    def weight_forward():
        for k in range(1, M):
            spot = wfull.at[2 * lax.rem(mine - k + M, M) + par]
            arrived(spot, wes.at[k], wer.at[k])
            send(spot, spot, wfs.at[k - 1], wfr.at[k - 1], partner)

    def weight_end():
        arrived(wfull.at[j + 1 - 2 * par], wes.at[0], wer.at[0])
        for k in range(1, M):
            spot = wfull.at[2 * lax.rem(mine - k + M, M) + 1 - par]
            arrived(spot, wfs.at[k - 1], wfr.at[k - 1])
        wsum_ref[...] = wfull[...]

    side = [weight_end, weight_forward, weight_spread, weight_node, weight_rep, weight_chip]

    def term(g, o):
        at = pl.ds(pl.multiple_of(o * rows, rows), rows)
        grads = rg[g].reshape(R * rows, gw)
        if has_t:
            return mm(dense_t[at, :], grads)
        return lax.dot_general(
            dense[:, at], grads, (((0,), (0,)), ((), ())), preferred_element_type=F32
        )

    pending = {}

    def ring_send(g, s, q, d):
        at = pl.ds(q * qr, qr)
        c = rcopy(
            rsb.at[g, s % D, d, at, :], rrb.at[g, s, d, at, :],
            rs.at[g, s, q, d], rr.at[g, s, q, d], (ring_to[d], j),
        )
        c.start()
        pending[(g, s, q, d)] = c

    def ring_event(g, s):
        if s == 0:
            tbuf[0] = term(g, node_at(h))
        else:
            for d in range(2):
                tbuf[d] = term(g, node_at(h - s if d == 0 else s - h))
        for q in range(Q):
            at = slice(q * qr, (q + 1) * qr)
            for d in range(2):
                if s == 0 and q not in half(d):
                    continue
                v = tbuf[0 if s == 0 else d, at, :]
                if s > 1 or (s == 1 and q in half(d)):
                    arrived(rrb.at[g, s - 1, d, pl.ds(q * qr, qr), :], rs.at[g, s - 1, q, d], rr.at[g, s - 1, q, d])
                    v += rrb[g, s - 1, d, at, :].astype(F32)
                if (g, s - D, q, d) in pending:
                    pending.pop((g, s - D, q, d)).wait_send()
                rsb[g, s % D, d, at, :] = v.astype(BF)
                ring_send(g, s, q, d)

    def ring_end(g):
        tbuf[0] = term(g, i)
        for q in range(Q):
            at = slice(q * qr, (q + 1) * qr)
            v = tbuf[0, at, :]
            for d in range(2):
                arrived(rrb.at[g, h - 1, d, pl.ds(q * qr, qr), :], rs.at[g, h - 1, q, d], rr.at[g, h - 1, q, d])
                v += rrb[g, h - 1, d, at, :].astype(F32)
            fg_ref[at, g * gw:(g + 1) * gw] = v.astype(BF)

    weight_terms()
    for g in range(G):
        for k in range(1, R):
            spot = rg.at[g, lax.rem(j - k + R, R)]
            arrived(spot, as_.at[g, k - 1], ar.at[g, k - 1])
        for s in range(h):
            ring_event(g, s)
            if s > 0 and len(side) > 1:
                side.pop()()
        if g == G - 1:
            while len(side) > 1:
                side.pop()()
        ring_end(g)
    side.pop()()

    for c in sent:
        c.wait_send()
    for c in pending.values():
        c.wait_send()


def plan_slots(tile_row, tile_col, tile_count, nodes, blocks, subs):
    cap = tile_row.shape[0]
    places = nodes * blocks * subs
    slot = jnp.arange(cap, dtype=jnp.int32)
    place = (tile_col // subs * blocks + tile_row) * subs + tile_col % subs
    place = jnp.where(slot < tile_count[0], place, places)
    key = place * cap + slot
    rank = jnp.sum((key[None, :] < key[:, None]).astype(jnp.int32), axis=1)
    sorted_key = jnp.sum(jnp.where(rank[None, :] == slot[:, None], key[None, :], 0), axis=1)
    spot = jnp.arange(places, dtype=jnp.int32)
    upto = jnp.sum((place[None, :] <= spot[:, None]).astype(jnp.int32), axis=1)
    there = jnp.sum((place[None, :] == spot[:, None]).astype(jnp.int32), axis=1)
    last = jnp.where(there > 0, upto - 1, cap)
    return sorted_key, last


def local(N, R, features, weight, cotangent, tile_values, tile_row, tile_col, tile_count):
    rows, F = features.shape
    cap = tile_values.shape[0]
    subs = rows // TB
    blocks = subs * R
    G, Q, T = 2, 4, 4
    gw, h = F // G, N // 2
    D = min(h, 4)
    qr = rows // Q
    wr = F // R
    pa = min(N, wr // 16)
    ph, pw = wr // pa, F // (N // pa)
    M = R // 2
    has_t = N * rows * rows * R * 2 <= 8 * 1024 * 1024
    sorted_key, last = plan_slots(tile_row, tile_col, tile_count, N, blocks, subs)
    cfg = (N, R, G, Q, D, T, cap, blocks, subs, has_t)
    dma = pltpu.SemaphoreType.DMA
    V = pltpu.VMEM
    scratch = [
        V((cap, TB, TB), BF), V((cap + 1, TB, TB), BF),
        V((R * rows, N * rows), BF),
        V((N * rows, R * rows) if has_t else (16, TB), BF),
        V((G, N * rows, gw), BF), V((G, R, rows, gw), F32),
        V((G, R - 1, rows, gw), BF), V((G, R - 1, rows, gw), BF),
        V((rows, F), BF), V((rows, F), F32), V((rows, F), BF), V((F, F), BF),
        V((G, R, rows, gw), BF), V((G, D, 2, rows, gw), BF), V((G, h, 2, rows, gw), BF),
        V((2, rows, gw), F32), V((F, rows), BF),
        V((R, wr, F), F32), V((R, wr, F), BF), V((M, wr, F), BF),
        V((max(M - 1, 1), wr, F), BF), V((max(M - 1, 1), wr, F), BF),
        V((wr, F), BF), V((N - 1, ph, pw), BF), V((R, wr, F), BF),
        dma((T,)), dma((G, h, Q, 2)), dma((G, h, Q, 2)),
        dma((G, R - 1)), dma((G, R - 1)), dma((G, R - 1)), dma((G, R - 1)),
        dma((G, h, Q, 2)), dma((G, h, Q, 2)),
        dma((M,)), dma((M,)), dma((M,)), dma((M,)),
        dma((N - 1,)), dma((N - 1,)), dma((N - 1,)), dma((N - 1,)),
        dma((M,)), dma((M,)), dma((M,)), dma((M,)),
    ]
    smem = pl.BlockSpec(memory_space=pltpu.SMEM)
    vmem = pl.BlockSpec(memory_space=pltpu.VMEM)
    act, wsum, feature_grad = pl.pallas_call(
        functools.partial(layer_kernel, cfg),
        out_shape=(
            jax.ShapeDtypeStruct((rows, F), BF),
            jax.ShapeDtypeStruct((R, wr, F), BF),
            jax.ShapeDtypeStruct((rows, F), BF),
        ),
        in_specs=[smem, smem, vmem, vmem, vmem, pl.BlockSpec(memory_space=pl.ANY)],
        out_specs=(vmem, vmem, vmem),
        scratch_shapes=scratch,
        compiler_params=pltpu.CompilerParams(
            collective_id=0, has_side_effects=True, vmem_limit_bytes=62 * 1024 * 1024
        ),
        name="layer",
    )(sorted_key, last, features, weight, cotangent, tile_values)
    scale = 1.0 / math.sqrt(rows * R * N)
    weight_grad = wsum.reshape(F, F).astype(F32) * scale
    return act, weight_grad, feature_grad


def solution(mesh):
    in_specs = (
        P(("node", "rep"), None),
        P(),
        P(("node", "rep"), None),
        P(("node", "rep"), None, None),
        P(("node", "rep")),
        P(("node", "rep")),
        P(("node", "rep")),
    )
    out_specs = (P(("node", "rep"), None), P(), P(("node", "rep"), None))
    step = functools.partial(local, mesh.shape["node"], mesh.shape["rep"])
    return jax.shard_map(step, mesh=mesh, in_specs=in_specs, out_specs=out_specs, check_vma=False)
```

```python
import functools
import math

import jax
import jax.numpy as jnp
from jax import lax
from jax.experimental import pallas as pl
from jax.experimental.pallas import tpu as pltpu
from jax.sharding import PartitionSpec as P

TB = 128
MESH = pl.DeviceIdType.MESH
BF = jnp.bfloat16
F32 = jnp.float32


def mm(a, b):
    return jnp.dot(a, b, preferred_element_type=F32)


def layer_kernel(
    cfg, count_ref, row_hbm, col_hbm, x_hbm, w_hbm, c_hbm, tiles_hbm,
    act_ref, wsum_ref, fg_ref,
    row_ref, col_ref, tiles, stage, dense, dense_t, X, part, psend, p1, p2s, p2, agg, pre, pg, w_ref, wt, c_ref,
    rg, rsb, rrb, tbuf, aggt, wterm, wsend, wa, wb, wbs, wq, wc, wfull,
    key_v, last_v, key_ref, last_ref,
    in_sem, tile_sem, plan_sem, gs, gr, p1s, p1r, p2ss, p2r, as_, ar, fs, fr, rs, rr,
    was, war, wbss, wbr, wcs, wcr, wds, wdr, wes, wer, wfs, wfr,
):
    N, R, G, D, T, cap, blocks, subs, has_t = cfg
    h, M = N // 2, R // 2
    rows, F = act_ref.shape
    gw = F // G
    hr, hw = rows // 2, gw // 2
    Q = 4
    i = lax.axis_index("node")
    j = lax.axis_index("rep")
    mine, par = lax.div(j, 2), lax.rem(j, 2)
    partner = (i, j + 1 - 2 * par)
    z, x = lax.div(i, 2), lax.rem(i, 2)
    pos = z + x * (N - 1 - 2 * z)

    def node_at(k):
        p = lax.rem(pos + (k + N), N)
        xx = lax.div(p, N // 2)
        return 2 * (p + xx * (N - 1 - 2 * p)) + xx

    right, left = node_at(1), node_at(-1)
    ring_to = (right, left)
    sent = []

    def rcopy(src, dst, ssem, rsem, dev):
        return pltpu.make_async_remote_copy(
            src_ref=src, dst_ref=dst, send_sem=ssem, recv_sem=rsem,
            device_id=dev, device_id_type=MESH,
        )

    def send(src, dst, ssem, rsem, dev):
        c = rcopy(src, dst, ssem, rsem, dev)
        c.start()
        sent.append(c)

    def arrived(dst, ssem, rsem):
        rcopy(dst, dst, ssem, rsem, (i, j)).wait_recv()

    def peer(k):
        return 2 * lax.rem(mine + k + M, M) + par

    def block(o):
        return pl.ds(pl.multiple_of(o * rows, rows), rows)

    def lanes(a):
        return pl.ds(a * hw, hw)

    def unit(q):
        return pl.ds(q % 2 * hr, hr), lanes(q // 2)

    def unit_of(o, q):
        return pl.ds(pl.multiple_of(o * rows + q % 2 * hr, hr), hr), lanes(q // 2)

    ins = [
        pltpu.make_async_copy(x_hbm.at[:, pl.ds(g * gw, gw)], X.at[g, block(i), :], in_sem.at[g])
        for g in range(G)
    ]
    ins.append(pltpu.make_async_copy(w_hbm, w_ref, in_sem.at[G]))
    ins.append(pltpu.make_async_copy(c_hbm, c_ref, in_sem.at[G + 1]))
    per = cap // T
    tile_copies = [
        pltpu.make_async_copy(
            tiles_hbm.at[pl.ds(k * per, per)], tiles.at[pl.ds(k * per, per)], tile_sem.at[k]
        )
        for k in range(T)
    ]
    spots = [
        pltpu.make_async_copy(row_hbm, row_ref, plan_sem.at[2]),
        pltpu.make_async_copy(col_hbm, col_ref, plan_sem.at[3]),
    ]
    for c in spots + ins + tile_copies:
        c.start()

    barrier = pltpu.get_barrier_semaphore()
    for n in ring_to:
        pl.semaphore_signal(barrier, inc=1, device_id=(n, j), device_id_type=MESH)
    for k in range(1, R):
        pl.semaphore_signal(barrier, inc=1, device_id=(i, lax.rem(j + k, R)), device_id_type=MESH)

    for c in spots:
        c.wait()
    places = N * blocks * subs
    slot_row = lax.broadcasted_iota(jnp.int32, (1, cap), 1)
    col = col_ref[...]
    place_row = (lax.div(col, subs) * blocks + row_ref[...]) * subs + lax.rem(col, subs)
    place_row = jnp.where(slot_row < count_ref[0], place_row, places)
    key_row = (place_row * cap + slot_row).astype(F32)
    down = lax.broadcasted_iota(jnp.int32, (cap, cap), 0)
    across = lax.broadcasted_iota(jnp.int32, (cap, cap), 1)
    keys = jnp.broadcast_to(key_row, (cap, cap))
    place_all = jnp.broadcast_to(place_row.astype(F32), (cap, cap))
    key_col = jnp.sum(jnp.where(down == across, keys, 0.0), axis=1, keepdims=True)
    place_col = jnp.sum(jnp.where(down == across, place_all, 0.0), axis=1, keepdims=True)
    rank = jnp.sum(jnp.where(keys < key_col, 1.0, 0.0), axis=1, keepdims=True)
    key_v[...] = jnp.sum(
        jnp.where(rank == across.astype(F32), key_col, 0.0), axis=0, keepdims=True
    ).astype(jnp.int32)
    spot = lax.broadcasted_iota(jnp.int32, (cap, places), 1).astype(F32)
    upto = jnp.sum(jnp.where(place_col <= spot, 1.0, 0.0), axis=0, keepdims=True)
    there = jnp.sum(jnp.where(place_col == spot, 1.0, 0.0), axis=0, keepdims=True)
    last_v[...] = jnp.where(there > 0.0, upto - 1.0, float(cap)).astype(jnp.int32)
    plan = [
        pltpu.make_async_copy(key_v, key_ref, plan_sem.at[0]),
        pltpu.make_async_copy(last_v, last_ref, plan_sem.at[1]),
    ]
    for c in plan:
        c.start()
    for g in range(G):
        ins[g].wait()
    pl.semaphore_wait(barrier, 2 + R - 1)

    def gather_send(g, s, q, d):
        at = (g,) + unit_of(node_at(-s if d == 0 else s), q)
        send(X.at[at], X.at[at], gs.at[g, s, q, d], gr.at[g, s, q, d], (ring_to[d], j))

    fresh = [[(g, q) for g in range(1, G) for q in range(Q)] for d in range(2)]

    def gather_event(g, s, q):
        for d in range(2):
            if s == h - 1 and q % 2 != d:
                continue
            at = (g,) + unit_of(node_at(-(s + 1) if d == 0 else s + 1), q)
            arrived(X.at[at], gs.at[g, s, q, d], gr.at[g, s, q, d])
            if s + 1 < h - 1 or (s + 1 == h - 1 and q % 2 == d):
                gather_send(g, s + 1, q, d)
            elif fresh[d]:
                fg, fq = fresh[d].pop(0)
                gather_send(fg, 0, fq, d)

    events = [(g, s, q) for g in range(G) for s in range(h) for q in range(Q)]
    events.reverse()

    def event_until(left):
        while len(events) > left:
            gather_event(*events.pop())

    for q in range(Q):
        for d in range(2):
            gather_send(0, 0, q, d)

    for c in ins[G:] + tile_copies + plan:
        c.wait()
    wt[...] = w_ref[...].T
    stage[cap] = jnp.zeros((TB, TB), BF)

    def slot_step(p, carry):
        acc, prev = carry
        key = jnp.maximum(key_ref[0, p], 0)
        slot = lax.rem(key, cap)
        place = lax.div(key, cap)
        keep = jnp.where(place == prev, 1.0, 0.0).astype(F32)
        acc = acc * keep + tiles[slot].astype(F32)
        stage[p] = acc.astype(BF)
        return acc, place

    group0 = (G - 1) * h * Q
    carry = (jnp.zeros((TB, TB), F32), jnp.int32(-1))
    for k in range(4):
        carry = lax.fori_loop(cap * k // 4, cap * (k + 1) // 4, slot_step, carry)
        event_until(max(group0, len(events) - 2))

    def place_step(o, carry):
        for r in range(blocks):
            for s in range(subs):
                tile = stage[jnp.clip(last_ref[0, (o * blocks + r) * subs + s], 0, cap)]
                at = pl.ds(pl.multiple_of((o * subs + s) * TB, TB), TB)
                dense[r * TB:(r + 1) * TB, at] = tile
                if has_t:
                    dense_t[at, r * TB:(r + 1) * TB] = tile.T
        return carry

    for k in range(2):
        lax.fori_loop(N * k // 2, N * (k + 1) // 2, place_step, 0)
        event_until(max(group0, len(events) - 2))
    event_until(group0)

    def chip_send(g, a, m, value):
        psend[g, m, :, a * hw:(a + 1) * hw] = value.astype(BF)
        at = (g, m, slice(None), lanes(a))
        send(psend.at[at], p1.at[at], p1s.at[g, a, m], p1r.at[g, a, m], partner)

    def chip_sum(g, a):
        at = slice(a * hw, (a + 1) * hw)
        for k in range(M - 1, -1, -1):
            m = lax.rem(mine + k, M)
            spot = p1.at[g, m, :, lanes(a)]
            arrived(spot, p1s.at[g, a, m], p1r.at[g, a, m])
            total = part[g, 2 * m + par, :, at] + p1[g, m, :, at].astype(F32)
            if k:
                p2s[g, k - 1, :, at] = total.astype(BF)
                spot = (g, k - 1, slice(None), lanes(a))
                send(p2s.at[spot], p2.at[spot], p2ss.at[g, a, k - 1], p2r.at[g, a, k - 1], (i, peer(k)))
            else:
                part[g, j, :, at] = total

    def rep_sum(g, a):
        at = slice(a * hw, (a + 1) * hw)
        total = part[g, j, :, at]
        for k in range(1, M):
            arrived(p2.at[g, k - 1, :, lanes(a)], p2ss.at[g, a, k - 1], p2r.at[g, a, k - 1])
            total += p2[g, k - 1, :, at].astype(F32)
        cols = slice(g * gw + a * hw, g * gw + (a + 1) * hw)
        agg[:, cols] = total.astype(BF)
        t = mm(agg[:, cols], w_ref[cols, :])
        pre[...] = t if g == 0 and a == 0 else pre[...] + t

    def block_part(g, offsets, first):
        def one(m, carry):
            total = None if first else part[g, m]
            for k in offsets:
                cols = block(node_at(k))
                t = mm(dense[block(m), cols], X[g, cols, :])
                total = t if total is None else total + t
            part[g, m] = total
            return carry

        lax.fori_loop(0, R, one, 0)

    for g in range(G):
        end = (G - 1 - g) * h * Q
        if g < G - 1:
            for m in range(M):
                jj = 2 * m + 1 - par
                value = mm(dense[block(jj), :], X[g])
                for a in range(2):
                    chip_send(g, a, m, value[:, a * hw:(a + 1) * hw])
                event_until(len(events) - 1)
            for m in range(M):
                jj = 2 * m + par
                part[g, jj] = mm(dense[block(jj), :], X[g])
                event_until(len(events) - 1)
            for a in range(2):
                chip_sum(g, a)
        else:
            block_part(g, [0], True)
            for s in range(h - 1):
                event_until((h - 1 - s) * Q)
                block_part(g, [-(s + 1), s + 1], False)
                if s == h - 2 and g > 0:
                    for a in range(2):
                        rep_sum(g - 1, a)
            cols = block(node_at(h))
            for a in range(2):
                at = slice(a * hw, (a + 1) * hw)
                event_until((1 - a) * Q // 2)
                for m in range(M):
                    jj = 2 * m + 1 - par
                    chip_send(g, a, m, part[g, jj, :, at] + mm(dense[block(jj), cols], X[g, cols, at]))
                for m in range(M):
                    jj = 2 * m + par
                    part[g, jj, :, at] = part[g, jj, :, at] + mm(dense[block(jj), cols], X[g, cols, at])
            for a in range(2):
                chip_sum(g, a)
            for a in range(2):
                rep_sum(g, a)

    root = math.sqrt(2.0 / math.pi)
    step = 64 if rows % 64 == 0 else rows

    def act_step(b, carry):
        at = pl.ds(pl.multiple_of(b * step, step), step)
        v = pre[at, :]
        v2 = v * v
        t = jnp.tanh(root * (v + 0.044715 * (v2 * v)))
        half_up = 0.5 * (1.0 + t)
        act_ref[at, :] = (v * half_up).astype(BF)
        slope = half_up + (0.5 * v) * (1.0 - t * t) * (root * (1.0 + (3 * 0.044715) * v2))
        pg[at, :] = (c_ref[at, :].astype(F32) * slope).astype(BF)
        return carry

    lax.fori_loop(0, rows // step, act_step, 0)

    def grad_at(g, jj, a):
        return rg.at[g, jj, :, lanes(a)]

    for g in range(G):
        for a in range(2):
            cols = slice(g * gw + a * hw, g * gw + (a + 1) * hw)
            rg[g, j, :, a * hw:(a + 1) * hw] = mm(pg[...], wt[:, cols]).astype(BF)
            spot = grad_at(g, j, a)
            for k in range(1, M):
                send(spot, spot, as_.at[g, a, k], ar.at[g, a, k], (i, peer(k)))
            send(spot, spot, as_.at[g, a, 0], ar.at[g, a, 0], partner)

    def grad_forward(g, a):
        for k in range(1, M):
            spot = grad_at(g, peer(-k), a)
            arrived(spot, as_.at[g, a, k], ar.at[g, a, k])
            send(spot, spot, fs.at[g, a, k - 1], fr.at[g, a, k - 1], partner)

    def grad_ready(g, a):
        arrived(grad_at(g, j + 1 - 2 * par, a), as_.at[g, a, 0], ar.at[g, a, 0])
        for k in range(1, M):
            spot = grad_at(g, peer(-k) + 1 - 2 * par, a)
            arrived(spot, fs.at[g, a, k - 1], fr.at[g, a, k - 1])

    wr = F // R
    pa = min(N, wr // 16)
    pb = N // pa
    ph, pw = wr // pa, F // pb

    def weight_terms():
        aggt[...] = agg[...].T

        def one(k, carry):
            at = pl.ds(pl.multiple_of(k * wr, wr), wr)
            t = mm(aggt[at, :], pg[...])
            wterm[k] = t
            wsend[k] = t.astype(BF)
            return carry

        lax.fori_loop(0, R, one, 0)
        for m in range(M):
            send(wsend.at[2 * m + 1 - par], wa.at[m], was.at[m], war.at[m], partner)

    def weight_chip():
        for m in range(M):
            arrived(wa.at[m], was.at[m], war.at[m])
            wterm[2 * m + par] = wterm[2 * m + par] + wa[m].astype(F32)
        for k in range(1, M):
            to = lax.rem(mine + k, M)
            wbs[k - 1] = wterm[2 * to + par].astype(BF)
            send(wbs.at[k - 1], wb.at[k - 1], wbss.at[k - 1], wbr.at[k - 1], (i, 2 * to + par))

    def piece(n):
        return (
            pl.ds(pl.multiple_of(lax.div(n, pb) * ph, ph), ph),
            pl.ds(pl.multiple_of(lax.rem(n, pb) * pw, pw), pw),
        )

    def weight_rep():
        total = wterm[j]
        for k in range(1, M):
            arrived(wb.at[k - 1], wbss.at[k - 1], wbr.at[k - 1])
            total += wb[k - 1].astype(F32)
        wq[...] = total.astype(BF)
        for k in range(1, N):
            n = lax.rem(i + k, N)
            send(wq.at[piece(n)], wc.at[k - 1], wcs.at[k - 1], wcr.at[k - 1], (n, j))

    def weight_node():
        at = piece(i)
        total = wq[at].astype(F32)
        for k in range(1, N):
            arrived(wc.at[k - 1], wcs.at[k - 1], wcr.at[k - 1])
            total += wc[k - 1].astype(F32)
        wfull[(j,) + at] = total.astype(BF)
        for k in range(1, N):
            spot = wfull.at[(j,) + at]
            send(spot, spot, wds.at[k - 1], wdr.at[k - 1], (lax.rem(i + k, N), j))

    def weight_spread():
        for k in range(1, N):
            spot = wfull.at[(j,) + piece(lax.rem(i - k + N, N))]
            arrived(spot, wds.at[k - 1], wdr.at[k - 1])
        quarter = wfull.at[j]
        for k in range(1, M):
            to = 2 * lax.rem(mine + k, M) + par
            send(quarter, quarter, wes.at[k], wer.at[k], (i, to))
        send(quarter, quarter, wes.at[0], wer.at[0], partner)

    def weight_forward():
        for k in range(1, M):
            spot = wfull.at[2 * lax.rem(mine - k + M, M) + par]
            arrived(spot, wes.at[k], wer.at[k])
            send(spot, spot, wfs.at[k - 1], wfr.at[k - 1], partner)

    def weight_end():
        arrived(wfull.at[j + 1 - 2 * par], wes.at[0], wer.at[0])
        for k in range(1, M):
            spot = wfull.at[2 * lax.rem(mine - k + M, M) + 1 - par]
            arrived(spot, wfs.at[k - 1], wfr.at[k - 1])
        wsum_ref[...] = wfull[...]

    side = [weight_end, weight_forward, weight_spread, weight_node, weight_rep, weight_chip]

    def term(g, o, at):
        grads = rg[g, :, :, at]
        grads = grads.reshape(R * rows, grads.shape[-1])
        if has_t:
            return mm(dense_t[block(o), :], grads)
        return lax.dot_general(
            dense[:, block(o)], grads, (((0,), (0,)), ((), ())), preferred_element_type=F32
        )

    pending = {}

    def ring_send(g, s, q, d):
        at = unit(q)
        c = rcopy(
            rsb.at[(g, s % D, d) + at], rrb.at[(g, s, d) + at],
            rs.at[g, s, q, d], rr.at[g, s, q, d], (ring_to[d], j),
        )
        c.start()
        pending[(g, s, q, d)] = c

    def cut(q):
        return slice(q % 2 * hr, (q % 2 + 1) * hr), slice(q // 2 * hw, (q // 2 + 1) * hw)

    def ring_unit(g, s, q, d, slot, incoming):
        v = tbuf[(slot,) + cut(q)]
        if incoming:
            arrived(rrb.at[(g, s - 1, d) + unit(q)], rs.at[g, s - 1, q, d], rr.at[g, s - 1, q, d])
            v += rrb[(g, s - 1, d) + cut(q)].astype(F32)
        if (g, s - D, q, d) in pending:
            pending.pop((g, s - D, q, d)).wait_send()
        rsb[(g, s % D, d) + cut(q)] = v.astype(BF)
        ring_send(g, s, q, d)

    def ring_event(g, s):
        if s == 0:
            for a in range(2):
                grad_forward(g, a)
                grad_ready(g, a)
                at = slice(a * hw, (a + 1) * hw)
                tbuf[0, :, at] = term(g, node_at(h), at)
                for d in range(2):
                    ring_unit(g, 0, 2 * a + d, d, 0, False)
            return
        for d in range(2):
            tbuf[d] = term(g, node_at(h - s if d == 0 else s - h), slice(None))
        order = [(q, d) for q in range(Q) for d in range(2)]
        if s == 1:
            order = [(q, d) for q, d in order if q % 2 != d] + [(q, d) for q, d in order if q % 2 == d]
        for q, d in order:
            ring_unit(g, s, q, d, d, s > 1 or q % 2 == d)

    def ring_end(g):
        tbuf[0] = term(g, i, slice(None))
        for q in range(Q):
            v = tbuf[(0,) + cut(q)]
            for d in range(2):
                arrived(rrb.at[(g, h - 1, d) + unit(q)], rs.at[g, h - 1, q, d], rr.at[g, h - 1, q, d])
                v += rrb[(g, h - 1, d) + cut(q)].astype(F32)
            r, c = cut(q)
            fg_ref[r, g * gw + c.start:g * gw + c.stop] = v.astype(BF)

    weight_terms()
    turns = []
    for g in range(G):
        turns += [(2 * (g * (h - 1) + s) + (g % 2), g, s) for s in range(h + 1)]
    turns.sort()
    for t, g, s in turns:
        if s < h:
            ring_event(g, s)
        else:
            ring_end(g)
        if len(side) > 1 and (g > 0 or s in (1, 3)):
            side.pop()()
    while side:
        side.pop()()

    for c in sent:
        c.wait_send()
    for c in pending.values():
        c.wait_send()


def finish_kernel(scale, act_in, wsum_in, fg_in, act_out, wg_out, fg_out, wide, sems):
    copies = [
        pltpu.make_async_copy(act_in, act_out, sems.at[0]),
        pltpu.make_async_copy(fg_in, fg_out, sems.at[1]),
    ]
    for c in copies:
        c.start()
    R, wr, F = wsum_in.shape
    for k in range(R):
        at = slice(k * wr, (k + 1) * wr)
        wide[at, :] = wsum_in[k].astype(F32) * scale
        c = pltpu.make_async_copy(wide.at[at, :], wg_out.at[at, :], sems.at[2 + k])
        c.start()
        copies.append(c)
    for c in copies:
        c.wait()


def local(N, R, features, weight, cotangent, tile_values, tile_row, tile_col, tile_count):
    rows, F = features.shape
    cap = tile_values.shape[0]
    subs = rows // TB
    blocks = subs * R
    G, T, Q = 2, 4, 4
    gw, h, M = F // G, N // 2, R // 2
    D = min(h, 4)
    wr = F // R
    pa = min(N, wr // 16)
    ph, pw = wr // pa, F // (N // pa)
    places = N * blocks * subs
    has_t = N * rows * rows * R * 2 <= 8 * 1024 * 1024
    cfg = (N, R, G, D, T, cap, blocks, subs, has_t)
    dma = pltpu.SemaphoreType.DMA
    V = pltpu.VMEM
    M1 = max(M - 1, 1)
    scratch = [
        V((1, cap), jnp.int32), V((1, cap), jnp.int32),
        V((cap, TB, TB), BF), V((cap + 1, TB, TB), BF),
        V((R * rows, N * rows), BF),
        V((N * rows, R * rows) if has_t else (16, TB), BF),
        V((G, N * rows, gw), BF), V((G, R, rows, gw), F32),
        V((G, M, rows, gw), BF), V((G, M, rows, gw), BF), V((G, M1, rows, gw), BF), V((G, M1, rows, gw), BF),
        V((rows, F), BF), V((rows, F), F32), V((rows, F), BF), V((F, F), BF), V((F, F), BF), V((rows, F), BF),
        V((G, R, rows, gw), BF), V((G, D, 2, rows, gw), BF), V((G, h, 2, rows, gw), BF),
        V((2, rows, gw), F32), V((F, rows), BF),
        V((R, wr, F), F32), V((R, wr, F), BF), V((M, wr, F), BF),
        V((M1, wr, F), BF), V((M1, wr, F), BF),
        V((wr, F), BF), V((N - 1, ph, pw), BF), V((R, wr, F), BF),
        V((1, cap), jnp.int32), V((1, places), jnp.int32),
        pltpu.SMEM((1, cap), jnp.int32), pltpu.SMEM((1, places), jnp.int32),
        dma((G + 2,)), dma((T,)), dma((4,)), dma((G, h, Q, 2)), dma((G, h, Q, 2)),
        dma((G, 2, M)), dma((G, 2, M)), dma((G, 2, M1)), dma((G, 2, M1)),
        dma((G, 2, M)), dma((G, 2, M)), dma((G, 2, M1)), dma((G, 2, M1)),
        dma((G, h, Q, 2)), dma((G, h, Q, 2)),
        dma((M,)), dma((M,)), dma((M,)), dma((M,)),
        dma((N - 1,)), dma((N - 1,)), dma((N - 1,)), dma((N - 1,)),
        dma((M,)), dma((M,)), dma((M,)), dma((M,)),
    ]
    smem = pl.BlockSpec(memory_space=pltpu.SMEM)
    vmem = pl.BlockSpec(memory_space=pltpu.VMEM)
    hbm = pl.BlockSpec(memory_space=pltpu.HBM)
    act, wsum, feature_grad = pl.pallas_call(
        functools.partial(layer_kernel, cfg),
        out_shape=(
            jax.ShapeDtypeStruct((rows, F), BF),
            jax.ShapeDtypeStruct((R, wr, F), BF),
            jax.ShapeDtypeStruct((rows, F), BF),
        ),
        in_specs=[smem] + [hbm] * 6,
        out_specs=(vmem, vmem, vmem),
        scratch_shapes=scratch,
        compiler_params=pltpu.CompilerParams(
            collective_id=0, has_side_effects=True,
            vmem_limit_bytes=(48 if has_t else 62) * 1024 * 1024,
        ),
        name="layer",
    )(
        tile_count,
        *(
            pltpu.with_memory_space_constraint(v, pltpu.HBM)
            for v in (
                tile_row.reshape(1, cap), tile_col.reshape(1, cap),
                features, weight, cotangent, tile_values,
            )
        ),
    )
    scale = 1.0 / math.sqrt(rows * R * N)
    act, weight_grad, feature_grad = pl.pallas_call(
        functools.partial(finish_kernel, scale),
        out_shape=(
            jax.ShapeDtypeStruct((rows, F), BF),
            jax.ShapeDtypeStruct((F, F), F32),
            jax.ShapeDtypeStruct((rows, F), BF),
        ),
        in_specs=[vmem, vmem, vmem],
        out_specs=(hbm, hbm, hbm),
        scratch_shapes=[V((F, F), F32), dma((2 + R,))],
        compiler_params=pltpu.CompilerParams(vmem_limit_bytes=8 * 1024 * 1024),
        name="finish",
    )(act, wsum, feature_grad)
    return act, weight_grad, feature_grad


def solution(mesh):
    in_specs = (
        P(("node", "rep"), None),
        P(),
        P(("node", "rep"), None),
        P(("node", "rep"), None, None),
        P(("node", "rep")),
        P(("node", "rep")),
        P(("node", "rep")),
    )
    out_specs = (P(("node", "rep"), None), P(), P(("node", "rep"), None))
    step = functools.partial(local, mesh.shape["node"], mesh.shape["rep"])
    return jax.shard_map(step, mesh=mesh, in_specs=in_specs, out_specs=out_specs, check_vma=False)
```

```python
import functools
import math

import jax
import jax.numpy as jnp
from jax import lax
from jax.experimental import pallas as pl
from jax.experimental.pallas import tpu as pltpu
from jax.sharding import PartitionSpec as P

TB = 128
FIRST = 2
SIDE_AT = (4, 12, 20, 25)
MESH = pl.DeviceIdType.MESH
BF = jnp.bfloat16
F32 = jnp.float32


def mm(a, b):
    return jnp.dot(a, b, preferred_element_type=F32)


def layer_kernel(
    cfg, count_ref, row_hbm, col_hbm, x_hbm, w_hbm, c_hbm, tiles_hbm,
    act_ref, wsum_ref, fg_ref,
    row_ref, col_ref, tiles, stage, dense, dense_t, X, part, psend, p1, p2s, p2, agg, pre, pg, w_ref, wt, c_ref,
    rg, rsb, rrb, tbuf, aggt, wterm, wsend, wa, wb, wbs, wq, wc, wfull,
    key_v, last_v, key_ref, last_ref,
    in_sem, tile_sem, plan_sem, gs, gr, p1s, p1r, p2ss, p2r, as_, ar, fs, fr, rs, rr,
    was, war, wbss, wbr, wcs, wcr, wds, wdr, wes, wer, wfs, wfr,
):
    N, R, G, D, T, cap, blocks, subs, has_t = cfg
    h, M = N // 2, R // 2
    rows, F = act_ref.shape
    gw = F // G
    hr, hw = rows // 2, gw // 2
    Q = 4
    i = lax.axis_index("node")
    j = lax.axis_index("rep")
    mine, par = lax.div(j, 2), lax.rem(j, 2)
    partner = (i, j + 1 - 2 * par)
    z, x = lax.div(i, 2), lax.rem(i, 2)
    pos = z + x * (N - 1 - 2 * z)

    def node_at(k):
        p = lax.rem(pos + (k + N), N)
        xx = lax.div(p, N // 2)
        return 2 * (p + xx * (N - 1 - 2 * p)) + xx

    right, left = node_at(1), node_at(-1)
    ring_to = (right, left)
    sent = []

    def rcopy(src, dst, ssem, rsem, dev):
        return pltpu.make_async_remote_copy(
            src_ref=src, dst_ref=dst, send_sem=ssem, recv_sem=rsem,
            device_id=dev, device_id_type=MESH,
        )

    def send(src, dst, ssem, rsem, dev):
        c = rcopy(src, dst, ssem, rsem, dev)
        c.start()
        sent.append(c)

    def arrived(dst, ssem, rsem):
        rcopy(dst, dst, ssem, rsem, (i, j)).wait_recv()

    def peer(k):
        return 2 * lax.rem(mine + k + M, M) + par

    def block(o):
        return pl.ds(pl.multiple_of(o * rows, rows), rows)

    def lanes(a):
        return pl.ds(a * hw, hw)

    def unit(q):
        return pl.ds(q % 2 * hr, hr), lanes(q // 2)

    def unit_of(o, q):
        return pl.ds(pl.multiple_of(o * rows + q % 2 * hr, hr), hr), lanes(q // 2)

    ins = [
        pltpu.make_async_copy(x_hbm.at[:, pl.ds(g * gw, gw)], X.at[g, block(i), :], in_sem.at[g])
        for g in range(G)
    ]
    ins.append(pltpu.make_async_copy(w_hbm, w_ref, in_sem.at[G]))
    ins.append(pltpu.make_async_copy(c_hbm, c_ref, in_sem.at[G + 1]))
    per = cap // T
    tile_copies = [
        pltpu.make_async_copy(
            tiles_hbm.at[pl.ds(k * per, per)], tiles.at[pl.ds(k * per, per)], tile_sem.at[k]
        )
        for k in range(T)
    ]
    spots = [
        pltpu.make_async_copy(row_hbm, row_ref, plan_sem.at[2]),
        pltpu.make_async_copy(col_hbm, col_ref, plan_sem.at[3]),
    ]
    for c in spots + ins + tile_copies:
        c.start()

    barrier = pltpu.get_barrier_semaphore()
    for n in ring_to:
        pl.semaphore_signal(barrier, inc=1, device_id=(n, j), device_id_type=MESH)
    for k in range(1, R):
        pl.semaphore_signal(barrier, inc=1, device_id=(i, lax.rem(j + k, R)), device_id_type=MESH)

    for g in range(G):
        ins[g].wait()
    pl.semaphore_wait(barrier, 2 + R - 1)

    def gather_send(g, s, q, d):
        at = (g,) + unit_of(node_at(-s if d == 0 else s), q)
        send(X.at[at], X.at[at], gs.at[g, s, q, d], gr.at[g, s, q, d], (ring_to[d], j))

    order, late = [(0, 0, q) for q in range(Q)], [(g, 0, q) for g in range(1, G) for q in range(Q)]
    order, late = order + late[:FIRST], late[FIRST:]
    first, events, n = list(order), [], 0
    while n < len(order):
        g, s, q = order[n]
        out = []
        if s + 1 < h - 1 or (s + 1 == h - 1 and q % 2 == 0):
            out.append((g, s + 1, q))
        if late and n >= 2:
            out.append(late.pop(0))
        order += out
        events.append(((g, s, q), out))
        n += 1
    events.reverse()

    def flip(q, d):
        return q - q % 2 + (q + d) % 2

    def event(count=1):
        for _ in range(min(count, len(events))):
            (g, s, q), out = events.pop()
            for d in range(2):
                at = (g,) + unit_of(node_at(-(s + 1) if d == 0 else s + 1), flip(q, d))
                arrived(X.at[at], gs.at[g, s, flip(q, d), d], gr.at[g, s, flip(q, d), d])
                for to in out:
                    gather_send(to[0], to[1], flip(to[2], d), d)

    def need(g, s, a):
        while any(e[0][0] == g and e[0][1] <= s and e[0][2] // 2 in a for e in events):
            event()

    for g, s, q in first:
        for d in range(2):
            gather_send(g, s, flip(q, d), d)

    for c in spots:
        c.wait()
    places = N * blocks * subs
    slot_row = lax.broadcasted_iota(jnp.int32, (1, cap), 1)
    col = col_ref[...]
    place_row = (lax.div(col, subs) * blocks + row_ref[...]) * subs + lax.rem(col, subs)
    place_row = jnp.where(slot_row < count_ref[0], place_row, places)
    key_row = (place_row * cap + slot_row).astype(F32)
    down = lax.broadcasted_iota(jnp.int32, (cap, cap), 0)
    across = lax.broadcasted_iota(jnp.int32, (cap, cap), 1)
    keys = jnp.broadcast_to(key_row, (cap, cap))
    place_all = jnp.broadcast_to(place_row.astype(F32), (cap, cap))
    key_col = jnp.sum(jnp.where(down == across, keys, 0.0), axis=1, keepdims=True)
    place_col = jnp.sum(jnp.where(down == across, place_all, 0.0), axis=1, keepdims=True)
    rank = jnp.sum(jnp.where(keys < key_col, 1.0, 0.0), axis=1, keepdims=True)
    key_v[...] = jnp.sum(
        jnp.where(rank == across.astype(F32), key_col, 0.0), axis=0, keepdims=True
    ).astype(jnp.int32)
    spot = lax.broadcasted_iota(jnp.int32, (cap, places), 1).astype(F32)
    upto = jnp.sum(jnp.where(place_col <= spot, 1.0, 0.0), axis=0, keepdims=True)
    there = jnp.sum(jnp.where(place_col == spot, 1.0, 0.0), axis=0, keepdims=True)
    last_v[...] = jnp.where(there > 0.0, upto - 1.0, float(cap)).astype(jnp.int32)
    plan = [
        pltpu.make_async_copy(key_v, key_ref, plan_sem.at[0]),
        pltpu.make_async_copy(last_v, last_ref, plan_sem.at[1]),
    ]
    for c in plan:
        c.start()
    for c in ins[G:] + tile_copies + plan:
        c.wait()
    wt[...] = w_ref[...].T
    stage[cap] = jnp.zeros((TB, TB), BF)

    def slot_step(p, carry):
        acc, prev = carry
        key = jnp.maximum(key_ref[0, p], 0)
        slot = lax.rem(key, cap)
        place = lax.div(key, cap)
        keep = jnp.where(place == prev, 1.0, 0.0).astype(F32)
        acc = acc * keep + tiles[slot].astype(F32)
        stage[p] = acc.astype(BF)
        return acc, place

    carry = (jnp.zeros((TB, TB), F32), jnp.int32(-1))
    for k in range(4):
        carry = lax.fori_loop(cap * k // 4, cap * (k + 1) // 4, slot_step, carry)
        event()

    def place_step(o, carry):
        for r in range(blocks):
            for s in range(subs):
                tile = stage[jnp.clip(last_ref[0, (o * blocks + r) * subs + s], 0, cap)]
                at = pl.ds(pl.multiple_of((o * subs + s) * TB, TB), TB)
                dense[r * TB:(r + 1) * TB, at] = tile
                if has_t:
                    dense_t[at, r * TB:(r + 1) * TB] = tile.T
        return carry

    for k in range(2):
        lax.fori_loop(N * k // 2, N * (k + 1) // 2, place_step, 0)
        event()

    def chip_send(g, a, m, value):
        psend[g, m, :, a * hw:(a + 1) * hw] = value.astype(BF)
        at = (g, m, slice(None), lanes(a))
        send(psend.at[at], p1.at[at], p1s.at[g, a, m], p1r.at[g, a, m], partner)

    def chip_sum(g, a):
        at = slice(a * hw, (a + 1) * hw)
        for k in range(M - 1, -1, -1):
            m = lax.rem(mine + k, M)
            spot = p1.at[g, m, :, lanes(a)]
            arrived(spot, p1s.at[g, a, m], p1r.at[g, a, m])
            total = part[g, 2 * m + par, :, at] + p1[g, m, :, at].astype(F32)
            if k:
                p2s[g, k - 1, :, at] = total.astype(BF)
                spot = (g, k - 1, slice(None), lanes(a))
                send(p2s.at[spot], p2.at[spot], p2ss.at[g, a, k - 1], p2r.at[g, a, k - 1], (i, peer(k)))
            else:
                part[g, j, :, at] = total

    def rep_sum(g, a):
        at = slice(a * hw, (a + 1) * hw)
        total = part[g, j, :, at]
        for k in range(1, M):
            arrived(p2.at[g, k - 1, :, lanes(a)], p2ss.at[g, a, k - 1], p2r.at[g, a, k - 1])
            total += p2[g, k - 1, :, at].astype(F32)
        cols = slice(g * gw + a * hw, g * gw + (a + 1) * hw)
        agg[:, cols] = total.astype(BF)
        t = mm(agg[:, cols], w_ref[cols, :])
        pre[...] = t if g == 0 and a == 0 else pre[...] + t

    def block_part(g, offsets, first):
        def one(m, carry):
            total = None if first else part[g, m]
            for k in offsets:
                cols = block(node_at(k))
                t = mm(dense[block(m), cols], X[g, cols, :])
                total = t if total is None else total + t
            part[g, m] = total
            return carry

        lax.fori_loop(0, R, one, 0)

    def last_block(g, a):
        cols = block(node_at(h))
        at = slice(a * hw, (a + 1) * hw)
        need(g, h - 1, (a,))
        for m in range(M):
            jj = 2 * m + 1 - par
            chip_send(g, a, m, part[g, jj, :, at] + mm(dense[block(jj), cols], X[g, cols, at]))
        for m in range(M):
            jj = 2 * m + par
            part[g, jj, :, at] = part[g, jj, :, at] + mm(dense[block(jj), cols], X[g, cols, at])

    for g in range(G):
        block_part(g, [0], True)
        event()
    for s in range(h - 1):
        for g in range(G):
            need(g, s, (0, 1))
            block_part(g, [-(s + 1), s + 1], False)
    halves = [(g, a) for g in range(G) for a in range(2)]
    for k, (g, a) in enumerate(halves):
        last_block(g, a)
        if k == len(halves) - 2:
            for done in halves[:-2]:
                chip_sum(*done)
    for done in halves[-2:]:
        chip_sum(*done)
    for done in halves:
        rep_sum(*done)

    root = math.sqrt(2.0 / math.pi)
    step = 64 if rows % 64 == 0 else rows

    def act_step(b, carry):
        at = pl.ds(pl.multiple_of(b * step, step), step)
        v = pre[at, :]
        v2 = v * v
        t = jnp.tanh(root * (v + 0.044715 * (v2 * v)))
        half_up = 0.5 * (1.0 + t)
        act_ref[at, :] = (v * half_up).astype(BF)
        slope = half_up + (0.5 * v) * (1.0 - t * t) * (root * (1.0 + (3 * 0.044715) * v2))
        pg[at, :] = (c_ref[at, :].astype(F32) * slope).astype(BF)
        return carry

    lax.fori_loop(0, rows // step, act_step, 0)

    def grad_at(g, jj, a):
        return rg.at[g, jj, :, lanes(a)]

    for g in range(G):
        for a in range(2):
            cols = slice(g * gw + a * hw, g * gw + (a + 1) * hw)
            rg[g, j, :, a * hw:(a + 1) * hw] = mm(pg[...], wt[:, cols]).astype(BF)
            spot = grad_at(g, j, a)
            for k in range(1, M):
                send(spot, spot, as_.at[g, a, k], ar.at[g, a, k], (i, peer(k)))
            send(spot, spot, as_.at[g, a, 0], ar.at[g, a, 0], partner)

    def grad_forward(g, a):
        for k in range(1, M):
            spot = grad_at(g, peer(-k), a)
            arrived(spot, as_.at[g, a, k], ar.at[g, a, k])
            send(spot, spot, fs.at[g, a, k - 1], fr.at[g, a, k - 1], partner)

    def grad_ready(g, a):
        arrived(grad_at(g, j + 1 - 2 * par, a), as_.at[g, a, 0], ar.at[g, a, 0])
        for k in range(1, M):
            spot = grad_at(g, peer(-k) + 1 - 2 * par, a)
            arrived(spot, fs.at[g, a, k - 1], fr.at[g, a, k - 1])

    wr = F // R
    pa = min(N, wr // 16)
    pb = N // pa
    ph, pw = wr // pa, F // pb

    def weight_terms():
        aggt[...] = agg[...].T

        def one(k, carry):
            at = pl.ds(pl.multiple_of(k * wr, wr), wr)
            t = mm(aggt[at, :], pg[...])
            wterm[k] = t
            wsend[k] = t.astype(BF)
            return carry

        lax.fori_loop(0, R, one, 0)
        for m in range(M):
            send(wsend.at[2 * m + 1 - par], wa.at[m], was.at[m], war.at[m], partner)

    def weight_chip():
        for m in range(M):
            arrived(wa.at[m], was.at[m], war.at[m])
            wterm[2 * m + par] = wterm[2 * m + par] + wa[m].astype(F32)
        for k in range(1, M):
            to = lax.rem(mine + k, M)
            wbs[k - 1] = wterm[2 * to + par].astype(BF)
            send(wbs.at[k - 1], wb.at[k - 1], wbss.at[k - 1], wbr.at[k - 1], (i, 2 * to + par))

    def piece(n):
        return (
            pl.ds(pl.multiple_of(lax.div(n, pb) * ph, ph), ph),
            pl.ds(pl.multiple_of(lax.rem(n, pb) * pw, pw), pw),
        )

    def weight_rep():
        total = wterm[j]
        for k in range(1, M):
            arrived(wb.at[k - 1], wbss.at[k - 1], wbr.at[k - 1])
            total += wb[k - 1].astype(F32)
        wq[...] = total.astype(BF)
        for k in range(1, N):
            n = lax.rem(i + k, N)
            send(wq.at[piece(n)], wc.at[k - 1], wcs.at[k - 1], wcr.at[k - 1], (n, j))

    def weight_node():
        at = piece(i)
        total = wq[at].astype(F32)
        for k in range(1, N):
            arrived(wc.at[k - 1], wcs.at[k - 1], wcr.at[k - 1])
            total += wc[k - 1].astype(F32)
        wfull[(j,) + at] = total.astype(BF)
        for k in range(1, N):
            spot = wfull.at[(j,) + at]
            send(spot, spot, wds.at[k - 1], wdr.at[k - 1], (lax.rem(i + k, N), j))

    def weight_spread():
        for k in range(1, N):
            spot = wfull.at[(j,) + piece(lax.rem(i - k + N, N))]
            arrived(spot, wds.at[k - 1], wdr.at[k - 1])
        quarter = wfull.at[j]
        for k in range(1, M):
            to = 2 * lax.rem(mine + k, M) + par
            send(quarter, quarter, wes.at[k], wer.at[k], (i, to))
        send(quarter, quarter, wes.at[0], wer.at[0], partner)

    def weight_forward():
        for k in range(1, M):
            spot = wfull.at[2 * lax.rem(mine - k + M, M) + par]
            arrived(spot, wes.at[k], wer.at[k])
            send(spot, spot, wfs.at[k - 1], wfr.at[k - 1], partner)

    def weight_end():
        arrived(wfull.at[j + 1 - 2 * par], wes.at[0], wer.at[0])
        for k in range(1, M):
            spot = wfull.at[2 * lax.rem(mine - k + M, M) + 1 - par]
            arrived(spot, wfs.at[k - 1], wfr.at[k - 1])
        wsum_ref[...] = wfull[...]

    side = [weight_end, weight_forward, weight_spread, weight_node, weight_rep, weight_chip]

    def term(g, o, at):
        grads = rg[g, :, :, at]
        grads = grads.reshape(R * rows, grads.shape[-1])
        if has_t:
            return mm(dense_t[block(o), :], grads)
        return lax.dot_general(
            dense[:, block(o)], grads, (((0,), (0,)), ((), ())), preferred_element_type=F32
        )

    pending = {}

    def ring_send(g, s, q, d):
        at = unit(q)
        c = rcopy(
            rsb.at[(g, s % D, d) + at], rrb.at[(g, s, d) + at],
            rs.at[g, s, q, d], rr.at[g, s, q, d], (ring_to[d], j),
        )
        c.start()
        pending[(g, s, q, d)] = c

    def cut(q):
        return slice(q % 2 * hr, (q % 2 + 1) * hr), slice(q // 2 * hw, (q // 2 + 1) * hw)

    made = set()

    def make(g, s, a):
        key = (g, s, a if s < 2 else 0)
        if key in made:
            return
        made.add(key)
        at = slice(a * hw, (a + 1) * hw) if s < 2 else slice(None)
        if s == 0 or s == h:
            tbuf[g, s % 3, 0, :, at] = term(g, node_at(h) if s == 0 else i, at)
        else:
            for d in range(2):
                tbuf[g, s % 3, d, :, at] = term(g, node_at(h - s if d == 0 else s - h), at)

    def come(g, s, q, d):
        arrived(rrb.at[(g, s, d) + unit(q)], rs.at[g, s, q, d], rr.at[g, s, q, d])
        return rrb[(g, s, d) + cut(q)].astype(F32)

    def ring_unit(g, s, u):
        make(g, s, u // 2)
        for d in range(2):
            q = flip(u, d)
            v = tbuf[(g, s % 3, d if s else 0) + cut(q)]
            if s > 1 or (s == 1 and u % 2 == 0):
                v += come(g, s - 1, q, d)
            if (g, s - D, q, d) in pending:
                pending.pop((g, s - D, q, d)).wait_send()
            rsb[(g, s % D, d) + cut(q)] = v.astype(BF)
            ring_send(g, s, q, d)

    def ring_end(g, a):
        make(g, h, a)
        for q in (2 * a, 2 * a + 1):
            v = tbuf[(g, h % 3, 0) + cut(q)]
            for d in range(2):
                v += come(g, h - 1, q, d)
            r, c = cut(q)
            fg_ref[r, g * gw + c.start:g * gw + c.stop] = v.astype(BF)

    weight_terms()
    order = []
    for g in range(G):
        for a in range(2):
            grad_forward(g, a)
            grad_ready(g, a)
            for s in range(2):
                ring_unit(g, s, 2 * a + s)
                order.append((g, s, 2 * a + s))
        if g == 0:
            side.pop()()
    n = 0
    while n < len(order):
        g, s, u = order[n]
        if s + 1 < h:
            ring_unit(g, s + 1, u)
            order.append((g, s + 1, u))
        elif all((g, s, u - u % 2 + k) in order[:n + 1] for k in range(2)):
            ring_end(g, u // 2)
        n += 1
        if n in SIDE_AT and len(side) > 1:
            side.pop()()
    while side:
        side.pop()()

    for c in sent:
        c.wait_send()
    for c in pending.values():
        c.wait_send()


def finish_kernel(scale, act_in, wsum_in, fg_in, act_out, wg_out, fg_out, wide, sems):
    copies = [
        pltpu.make_async_copy(act_in, act_out, sems.at[0]),
        pltpu.make_async_copy(fg_in, fg_out, sems.at[1]),
    ]
    for c in copies:
        c.start()
    R, wr, F = wsum_in.shape
    for k in range(R):
        at = slice(k * wr, (k + 1) * wr)
        wide[at, :] = wsum_in[k].astype(F32) * scale
        c = pltpu.make_async_copy(wide.at[at, :], wg_out.at[at, :], sems.at[2 + k])
        c.start()
        copies.append(c)
    for c in copies:
        c.wait()


def local(N, R, features, weight, cotangent, tile_values, tile_row, tile_col, tile_count):
    rows, F = features.shape
    cap = tile_values.shape[0]
    subs = rows // TB
    blocks = subs * R
    G, T, Q = 2, 4, 4
    gw, h, M = F // G, N // 2, R // 2
    D = min(h, 4)
    wr = F // R
    pa = min(N, wr // 16)
    ph, pw = wr // pa, F // (N // pa)
    places = N * blocks * subs
    has_t = N * rows * rows * R * 2 <= 8 * 1024 * 1024
    cfg = (N, R, G, D, T, cap, blocks, subs, has_t)
    dma = pltpu.SemaphoreType.DMA
    V = pltpu.VMEM
    M1 = max(M - 1, 1)
    scratch = [
        V((1, cap), jnp.int32), V((1, cap), jnp.int32),
        V((cap, TB, TB), BF), V((cap + 1, TB, TB), BF),
        V((R * rows, N * rows), BF),
        V((N * rows, R * rows) if has_t else (16, TB), BF),
        V((G, N * rows, gw), BF), V((G, R, rows, gw), F32),
        V((G, M, rows, gw), BF), V((G, M, rows, gw), BF), V((G, M1, rows, gw), BF), V((G, M1, rows, gw), BF),
        V((rows, F), BF), V((rows, F), F32), V((rows, F), BF), V((F, F), BF), V((F, F), BF), V((rows, F), BF),
        V((G, R, rows, gw), BF), V((G, D, 2, rows, gw), BF), V((G, h, 2, rows, gw), BF),
        V((G, 3, 2, rows, gw), F32), V((F, rows), BF),
        V((R, wr, F), F32), V((R, wr, F), BF), V((M, wr, F), BF),
        V((M1, wr, F), BF), V((M1, wr, F), BF),
        V((wr, F), BF), V((N - 1, ph, pw), BF), V((R, wr, F), BF),
        V((1, cap), jnp.int32), V((1, places), jnp.int32),
        pltpu.SMEM((1, cap), jnp.int32), pltpu.SMEM((1, places), jnp.int32),
        dma((G + 2,)), dma((T,)), dma((4,)), dma((G, h, Q, 2)), dma((G, h, Q, 2)),
        dma((G, 2, M)), dma((G, 2, M)), dma((G, 2, M1)), dma((G, 2, M1)),
        dma((G, 2, M)), dma((G, 2, M)), dma((G, 2, M1)), dma((G, 2, M1)),
        dma((G, h, Q, 2)), dma((G, h, Q, 2)),
        dma((M,)), dma((M,)), dma((M,)), dma((M,)),
        dma((N - 1,)), dma((N - 1,)), dma((N - 1,)), dma((N - 1,)),
        dma((M,)), dma((M,)), dma((M,)), dma((M,)),
    ]
    smem = pl.BlockSpec(memory_space=pltpu.SMEM)
    vmem = pl.BlockSpec(memory_space=pltpu.VMEM)
    hbm = pl.BlockSpec(memory_space=pltpu.HBM)
    act, wsum, feature_grad = pl.pallas_call(
        functools.partial(layer_kernel, cfg),
        out_shape=(
            jax.ShapeDtypeStruct((rows, F), BF),
            jax.ShapeDtypeStruct((R, wr, F), BF),
            jax.ShapeDtypeStruct((rows, F), BF),
        ),
        in_specs=[smem] + [hbm] * 6,
        out_specs=(vmem, vmem, vmem),
        scratch_shapes=scratch,
        compiler_params=pltpu.CompilerParams(
            collective_id=0, has_side_effects=True,
            vmem_limit_bytes=(48 if has_t else 63) * 1024 * 1024,
        ),
        name="layer",
    )(
        tile_count,
        *(
            pltpu.with_memory_space_constraint(v, pltpu.HBM)
            for v in (
                tile_row.reshape(1, cap), tile_col.reshape(1, cap),
                features, weight, cotangent, tile_values,
            )
        ),
    )
    scale = 1.0 / math.sqrt(rows * R * N)
    act, weight_grad, feature_grad = pl.pallas_call(
        functools.partial(finish_kernel, scale),
        out_shape=(
            jax.ShapeDtypeStruct((rows, F), BF),
            jax.ShapeDtypeStruct((F, F), F32),
            jax.ShapeDtypeStruct((rows, F), BF),
        ),
        in_specs=[vmem, vmem, vmem],
        out_specs=(hbm, hbm, hbm),
        scratch_shapes=[V((F, F), F32), dma((2 + R,))],
        compiler_params=pltpu.CompilerParams(vmem_limit_bytes=8 * 1024 * 1024),
        name="finish",
    )(act, wsum, feature_grad)
    return act, weight_grad, feature_grad


def solution(mesh):
    in_specs = (
        P(("node", "rep"), None),
        P(),
        P(("node", "rep"), None),
        P(("node", "rep"), None, None),
        P(("node", "rep")),
        P(("node", "rep")),
        P(("node", "rep")),
    )
    out_specs = (P(("node", "rep"), None), P(), P(("node", "rep"), None))
    step = functools.partial(local, mesh.shape["node"], mesh.shape["rep"])
    return jax.shard_map(step, mesh=mesh, in_specs=in_specs, out_specs=out_specs, check_vma=False)
```

```python
import functools
import math

import jax
import jax.numpy as jnp
from jax import lax
from jax.experimental import pallas as pl
from jax.experimental.pallas import tpu as pltpu
from jax.sharding import PartitionSpec as P

TB = 128
FIRST = 4
SIDE_AT = (2, 6, 10, 17, 23)
MESH = pl.DeviceIdType.MESH
BF = jnp.bfloat16
F32 = jnp.float32


def mm(a, b):
    return jnp.dot(a, b, preferred_element_type=F32)


def layer_kernel(
    cfg, count_ref, row_hbm, col_hbm, x_hbm, w_hbm, c_hbm, tiles_hbm,
    act_ref, wsum_ref, fg_ref,
    row_ref, col_ref, tiles, stage, dense, dense_t, X, part, psend, p1, p2s, p2, agg, pre, pg, w_ref, wt, c_ref,
    rg, rsb, rrb, tbuf, aggt, wterm, wsend, wa, wb, wbs, wxs, wx, wq, wc, wfull,
    key_v, last_v, key_ref, last_ref,
    in_sem, tile_sem, plan_sem, gs, gr, p1s, p1r, p2ss, p2r, as_, ar, fs, fr, rs, rr,
    was, war, wbss, wbr, wxsem, wcs, wcr, wds, wdr, wes, wer, wfs, wfr,
):
    N, R, G, D, T, cap, blocks, subs, has_t = cfg
    h, M = N // 2, R // 2
    rows, F = act_ref.shape
    gw = F // G
    hr, hw = rows // 2, gw // 2
    Q = 4
    i = lax.axis_index("node")
    j = lax.axis_index("rep")
    mine, par = lax.div(j, 2), lax.rem(j, 2)
    partner = (i, j + 1 - 2 * par)
    z, x = lax.div(i, 2), lax.rem(i, 2)
    pos = z + x * (N - 1 - 2 * z)

    def node_at(k):
        p = lax.rem(pos + (k + N), N)
        xx = lax.div(p, N // 2)
        return 2 * (p + xx * (N - 1 - 2 * p)) + xx

    right, left = node_at(1), node_at(-1)
    ring_to = (right, left)
    sent = []

    def rcopy(src, dst, ssem, rsem, dev):
        return pltpu.make_async_remote_copy(
            src_ref=src, dst_ref=dst, send_sem=ssem, recv_sem=rsem,
            device_id=dev, device_id_type=MESH,
        )

    def send(src, dst, ssem, rsem, dev):
        c = rcopy(src, dst, ssem, rsem, dev)
        c.start()
        sent.append(c)

    def arrived(dst, ssem, rsem):
        rcopy(dst, dst, ssem, rsem, (i, j)).wait_recv()

    def peer(k):
        return 2 * lax.rem(mine + k + M, M) + par

    def block(o):
        return pl.ds(pl.multiple_of(o * rows, rows), rows)

    def lanes(a):
        return pl.ds(a * hw, hw)

    def unit(q):
        return pl.ds(q % 2 * hr, hr), lanes(q // 2)

    def unit_of(o, q):
        return pl.ds(pl.multiple_of(o * rows + q % 2 * hr, hr), hr), lanes(q // 2)

    ins = [
        pltpu.make_async_copy(x_hbm.at[:, pl.ds(g * gw, gw)], X.at[g, block(i), :], in_sem.at[g])
        for g in range(G)
    ]
    ins.append(pltpu.make_async_copy(w_hbm, w_ref, in_sem.at[G]))
    ins.append(pltpu.make_async_copy(c_hbm, c_ref, in_sem.at[G + 1]))
    per = cap // T
    tile_copies = [
        pltpu.make_async_copy(
            tiles_hbm.at[pl.ds(k * per, per)], tiles.at[pl.ds(k * per, per)], tile_sem.at[k]
        )
        for k in range(T)
    ]
    spots = [
        pltpu.make_async_copy(row_hbm, row_ref, plan_sem.at[2]),
        pltpu.make_async_copy(col_hbm, col_ref, plan_sem.at[3]),
    ]
    for c in spots + ins + tile_copies:
        c.start()

    barrier = pltpu.get_barrier_semaphore()
    for n in ring_to:
        pl.semaphore_signal(barrier, inc=1, device_id=(n, j), device_id_type=MESH)
    for k in range(1, R):
        pl.semaphore_signal(barrier, inc=1, device_id=(i, lax.rem(j + k, R)), device_id_type=MESH)

    for g in range(G):
        ins[g].wait()
    pl.semaphore_wait(barrier, 2 + R - 1)

    def gather_send(g, s, q, d):
        at = (g,) + unit_of(node_at(-s if d == 0 else s), q)
        send(X.at[at], X.at[at], gs.at[g, s, q, d], gr.at[g, s, q, d], (ring_to[d], j))

    order, late = [(0, 0, q) for q in range(Q)], [(g, 0, q) for g in range(1, G) for q in range(Q)]
    order, late = order + late[:FIRST], late[FIRST:]
    first, events, n = list(order), [], 0
    while n < len(order):
        g, s, q = order[n]
        out = []
        if s + 1 < h - 1 or (s + 1 == h - 1 and q % 2 == 0):
            out.append((g, s + 1, q))
        if late and n >= 2:
            out.append(late.pop(0))
        order += out
        events.append(((g, s, q), out))
        n += 1
    events.reverse()

    def flip(q, d):
        return q - q % 2 + (q + d) % 2

    def event(count=1):
        for _ in range(min(count, len(events))):
            (g, s, q), out = events.pop()
            for d in range(2):
                at = (g,) + unit_of(node_at(-(s + 1) if d == 0 else s + 1), flip(q, d))
                arrived(X.at[at], gs.at[g, s, flip(q, d), d], gr.at[g, s, flip(q, d), d])
                for to in out:
                    gather_send(to[0], to[1], flip(to[2], d), d)

    def need(g, s, a):
        while any(e[0][0] == g and e[0][1] <= s and e[0][2] // 2 in a for e in events):
            event()

    for g, s, q in first:
        for d in range(2):
            gather_send(g, s, flip(q, d), d)

    for c in spots:
        c.wait()
    places = N * blocks * subs
    slot_row = lax.broadcasted_iota(jnp.int32, (1, cap), 1)
    col = col_ref[...]
    place_row = (lax.div(col, subs) * blocks + row_ref[...]) * subs + lax.rem(col, subs)
    place_row = jnp.where(slot_row < count_ref[0], place_row, places)
    key_row = (place_row * cap + slot_row).astype(F32)
    down = lax.broadcasted_iota(jnp.int32, (cap, cap), 0)
    across = lax.broadcasted_iota(jnp.int32, (cap, cap), 1)
    keys = jnp.broadcast_to(key_row, (cap, cap))
    place_all = jnp.broadcast_to(place_row.astype(F32), (cap, cap))
    key_col = jnp.sum(jnp.where(down == across, keys, 0.0), axis=1, keepdims=True)
    place_col = jnp.sum(jnp.where(down == across, place_all, 0.0), axis=1, keepdims=True)
    rank = jnp.sum(jnp.where(keys < key_col, 1.0, 0.0), axis=1, keepdims=True)
    key_v[...] = jnp.sum(
        jnp.where(rank == across.astype(F32), key_col, 0.0), axis=0, keepdims=True
    ).astype(jnp.int32)
    spot = lax.broadcasted_iota(jnp.int32, (cap, places), 1).astype(F32)
    upto = jnp.sum(jnp.where(place_col <= spot, 1.0, 0.0), axis=0, keepdims=True)
    there = jnp.sum(jnp.where(place_col == spot, 1.0, 0.0), axis=0, keepdims=True)
    last_v[...] = jnp.where(there > 0.0, upto - 1.0, float(cap)).astype(jnp.int32)
    plan = [
        pltpu.make_async_copy(key_v, key_ref, plan_sem.at[0]),
        pltpu.make_async_copy(last_v, last_ref, plan_sem.at[1]),
    ]
    for c in plan:
        c.start()
    for c in ins[G:] + tile_copies + plan:
        c.wait()
    wt[...] = w_ref[...].T
    stage[cap] = jnp.zeros((TB, TB), BF)

    def slot_step(p, carry):
        acc, prev = carry
        key = jnp.maximum(key_ref[0, p], 0)
        slot = lax.rem(key, cap)
        place = lax.div(key, cap)
        keep = jnp.where(place == prev, 1.0, 0.0).astype(F32)
        acc = acc * keep + tiles[slot].astype(F32)
        stage[p] = acc.astype(BF)
        return acc, place

    carry = (jnp.zeros((TB, TB), F32), jnp.int32(-1))
    for k in range(4):
        carry = lax.fori_loop(cap * k // 4, cap * (k + 1) // 4, slot_step, carry)
        event()

    def place_step(o, carry):
        for r in range(blocks):
            for s in range(subs):
                tile = stage[jnp.clip(last_ref[0, (o * blocks + r) * subs + s], 0, cap)]
                at = pl.ds(pl.multiple_of((o * subs + s) * TB, TB), TB)
                dense[r * TB:(r + 1) * TB, at] = tile
                if has_t:
                    dense_t[at, r * TB:(r + 1) * TB] = tile.T
        return carry

    for k in range(2):
        lax.fori_loop(N * k // 2, N * (k + 1) // 2, place_step, 0)
        event()

    def chip_send(g, a, m, value):
        psend[g, m, :, a * hw:(a + 1) * hw] = value.astype(BF)
        at = (g, m, slice(None), lanes(a))
        send(psend.at[at], p1.at[at], p1s.at[g, a, m], p1r.at[g, a, m], partner)

    def chip_sum(g, a):
        at = slice(a * hw, (a + 1) * hw)
        for k in range(M - 1, -1, -1):
            m = lax.rem(mine + k, M)
            spot = p1.at[g, m, :, lanes(a)]
            arrived(spot, p1s.at[g, a, m], p1r.at[g, a, m])
            total = part[g, 2 * m + par, :, at] + p1[g, m, :, at].astype(F32)
            if k:
                p2s[g, k - 1, :, at] = total.astype(BF)
                spot = (g, k - 1, slice(None), lanes(a))
                send(p2s.at[spot], p2.at[spot], p2ss.at[g, a, k - 1], p2r.at[g, a, k - 1], (i, peer(k)))
            else:
                part[g, j, :, at] = total

    def rep_sum(g, a):
        at = slice(a * hw, (a + 1) * hw)
        total = part[g, j, :, at]
        for k in range(1, M):
            arrived(p2.at[g, k - 1, :, lanes(a)], p2ss.at[g, a, k - 1], p2r.at[g, a, k - 1])
            total += p2[g, k - 1, :, at].astype(F32)
        cols = slice(g * gw + a * hw, g * gw + (a + 1) * hw)
        agg[:, cols] = total.astype(BF)
        t = mm(agg[:, cols], w_ref[cols, :])
        pre[...] = t if g == 0 and a == 0 else pre[...] + t

    def block_part(g, offsets, first):
        def one(m, carry):
            total = None if first else part[g, m]
            for k in offsets:
                cols = block(node_at(k))
                t = mm(dense[block(m), cols], X[g, cols, :])
                total = t if total is None else total + t
            part[g, m] = total
            return carry

        lax.fori_loop(0, R, one, 0)

    def last_block(g, a):
        cols = block(node_at(h))
        at = slice(a * hw, (a + 1) * hw)
        need(g, h - 1, (a,))
        for m in range(M):
            jj = 2 * m + 1 - par
            chip_send(g, a, m, part[g, jj, :, at] + mm(dense[block(jj), cols], X[g, cols, at]))
        for m in range(M):
            jj = 2 * m + par
            part[g, jj, :, at] = part[g, jj, :, at] + mm(dense[block(jj), cols], X[g, cols, at])

    for g in range(G):
        block_part(g, [0], True)
        event()
    for s in range(h - 1):
        for g in range(G):
            need(g, s, (0, 1))
            block_part(g, [-(s + 1), s + 1], False)
    halves = [(g, a) for g in range(G) for a in range(2)]
    for k, (g, a) in enumerate(halves):
        last_block(g, a)
        if k == len(halves) - 2:
            for done in halves[:-1]:
                chip_sum(*done)
    for done in halves[-1:]:
        chip_sum(*done)
    for done in halves:
        rep_sum(*done)

    root = math.sqrt(2.0 / math.pi)
    step = 64 if rows % 64 == 0 else rows

    def act_step(b, carry):
        at = pl.ds(pl.multiple_of(b * step, step), step)
        v = pre[at, :]
        v2 = v * v
        t = jnp.tanh(root * (v + 0.044715 * (v2 * v)))
        half_up = 0.5 * (1.0 + t)
        act_ref[at, :] = (v * half_up).astype(BF)
        slope = half_up + (0.5 * v) * (1.0 - t * t) * (root * (1.0 + (3 * 0.044715) * v2))
        pg[at, :] = (c_ref[at, :].astype(F32) * slope).astype(BF)
        return carry

    lax.fori_loop(0, rows // step, act_step, 0)

    def grad_at(g, jj, a):
        return rg.at[g, jj, :, lanes(a)]

    for g in range(G):
        for a in range(2):
            cols = slice(g * gw + a * hw, g * gw + (a + 1) * hw)
            rg[g, j, :, a * hw:(a + 1) * hw] = mm(pg[...], wt[:, cols]).astype(BF)
            spot = grad_at(g, j, a)
            for k in range(1, M):
                send(spot, spot, as_.at[g, a, k], ar.at[g, a, k], (i, peer(k)))
            send(spot, spot, as_.at[g, a, 0], ar.at[g, a, 0], partner)

    def grad_forward(g, a):
        for k in range(1, M):
            spot = grad_at(g, peer(-k), a)
            arrived(spot, as_.at[g, a, k], ar.at[g, a, k])
            send(spot, spot, fs.at[g, a, k - 1], fr.at[g, a, k - 1], partner)

    def grad_ready(g, a):
        arrived(grad_at(g, j + 1 - 2 * par, a), as_.at[g, a, 0], ar.at[g, a, 0])
        for k in range(1, M):
            spot = grad_at(g, peer(-k) + 1 - 2 * par, a)
            arrived(spot, fs.at[g, a, k - 1], fr.at[g, a, k - 1])

    wr = F // R
    Z, hx = N // 2, wr // 2
    pa = min(Z, hx // 16)
    pb = Z // pa
    ph, pw = hx // pa, F // pb

    def weight_terms():
        aggt[...] = agg[...].T

        def one(k, carry):
            at = pl.ds(pl.multiple_of(k * wr, wr), wr)
            t = mm(aggt[at, :], pg[...])
            wterm[k] = t
            wsend[k] = t.astype(BF)
            return carry

        lax.fori_loop(0, R, one, 0)
        for m in range(M):
            send(wsend.at[2 * m + 1 - par], wa.at[m], was.at[m], war.at[m], partner)

    def weight_chip():
        for m in range(M):
            arrived(wa.at[m], was.at[m], war.at[m])
            wterm[2 * m + par] = wterm[2 * m + par] + wa[m].astype(F32)
        for k in range(1, M):
            to = lax.rem(mine + k, M)
            wbs[k - 1] = wterm[2 * to + par].astype(BF)
            send(wbs.at[k - 1], wb.at[k - 1], wbss.at[k - 1], wbr.at[k - 1], (i, 2 * to + par))

    across_node = (i + 1 - 2 * x, j)

    def half_rows(b):
        return pl.ds(pl.multiple_of(b * hx, hx), hx)

    def other(k):
        return lax.rem(z + k + Z, Z)

    def piece(n, base):
        return (
            pl.ds(pl.multiple_of(base + lax.div(n, pb) * ph, ph), ph),
            pl.ds(pl.multiple_of(lax.rem(n, pb) * pw, pw), pw),
        )

    def weight_rep():
        for b in (1 - x, x):
            total = wterm[j, half_rows(b), :]
            for k in range(1, M):
                if b is not x:
                    arrived(wb.at[k - 1], wbss.at[k - 1], wbr.at[k - 1])
                total += wb[k - 1, half_rows(b), :].astype(F32)
            if b is x:
                wterm[j, half_rows(b), :] = total
            else:
                wxs[...] = total.astype(BF)
                send(wxs, wx, wxsem.at[0], wxsem.at[1], across_node)

    def weight_pair():
        arrived(wx, wxsem.at[0], wxsem.at[1])
        wq[...] = (wterm[j, half_rows(x), :] + wx[...].astype(F32)).astype(BF)
        for k in range(1, Z):
            n = other(k)
            send(wq.at[piece(n, 0)], wc.at[k - 1], wcs.at[k - 1], wcr.at[k - 1], (2 * n + x, j))

    def weight_node():
        total = wq[piece(z, 0)].astype(F32)
        for k in range(1, Z):
            arrived(wc.at[k - 1], wcs.at[k - 1], wcr.at[k - 1])
            total += wc[k - 1].astype(F32)
        at = (j,) + piece(z, x * hx)
        wfull[at] = total.astype(BF)
        for k in range(1, N):
            send(wfull.at[at], wfull.at[at], wds.at[k - 1], wdr.at[k - 1], (lax.rem(i + k, N), j))

    def weight_spread():
        for k in range(1, N):
            n = lax.rem(i - k + N, N)
            at = (j,) + piece(lax.div(n, 2), lax.rem(n, 2) * hx)
            arrived(wfull.at[at], wds.at[k - 1], wdr.at[k - 1])
        spot = wfull.at[j]
        for k in range(1, M):
            send(spot, spot, wes.at[k], wer.at[k], (i, peer(k)))
        send(spot, spot, wes.at[0], wer.at[0], partner)

    def weight_forward():
        for k in range(1, M):
            spot = wfull.at[peer(-k)]
            arrived(spot, wes.at[k], wer.at[k])
            send(spot, spot, wfs.at[k - 1], wfr.at[k - 1], partner)

    def weight_end():
        arrived(wfull.at[j + 1 - 2 * par], wes.at[0], wer.at[0])
        for k in range(1, M):
            spot = wfull.at[peer(-k) + 1 - 2 * par]
            arrived(spot, wfs.at[k - 1], wfr.at[k - 1])
        wsum_ref[...] = wfull[...]

    side = [
        weight_end, weight_forward, weight_spread,
        weight_node, weight_pair, weight_rep, weight_chip,
    ]

    def term(g, o, at):
        grads = rg[g, :, :, at]
        grads = grads.reshape(R * rows, grads.shape[-1])
        if has_t:
            return mm(dense_t[block(o), :], grads)
        return lax.dot_general(
            dense[:, block(o)], grads, (((0,), (0,)), ((), ())), preferred_element_type=F32
        )

    pending = {}

    def ring_send(g, s, q, d):
        at = unit(q)
        c = rcopy(
            rsb.at[(g, s % D, d) + at], rrb.at[(g, s, d) + at],
            rs.at[g, s, q, d], rr.at[g, s, q, d], (ring_to[d], j),
        )
        c.start()
        pending[(g, s, q, d)] = c

    def cut(q):
        return slice(q % 2 * hr, (q % 2 + 1) * hr), slice(q // 2 * hw, (q // 2 + 1) * hw)

    made = set()

    def make(g, s, a):
        key = (g, s, a if s < 2 else 0)
        if key in made:
            return
        made.add(key)
        at = slice(a * hw, (a + 1) * hw) if s < 2 else slice(None)
        if s == 0 or s == h:
            tbuf[g, s % 3, 0, :, at] = term(g, node_at(h) if s == 0 else i, at)
        else:
            for d in range(2):
                tbuf[g, s % 3, d, :, at] = term(g, node_at(h - s if d == 0 else s - h), at)

    def come(g, s, q, d):
        arrived(rrb.at[(g, s, d) + unit(q)], rs.at[g, s, q, d], rr.at[g, s, q, d])
        return rrb[(g, s, d) + cut(q)].astype(F32)

    def ring_unit(g, s, u):
        make(g, s, u // 2)
        for d in range(2):
            q = flip(u, d)
            v = tbuf[(g, s % 3, d if s else 0) + cut(q)]
            if s > 1 or (s == 1 and u % 2 == 0):
                v += come(g, s - 1, q, d)
            if (g, s - D, q, d) in pending:
                pending.pop((g, s - D, q, d)).wait_send()
            rsb[(g, s % D, d) + cut(q)] = v.astype(BF)
            ring_send(g, s, q, d)

    def ring_end(g, a):
        make(g, h, a)
        for q in (2 * a, 2 * a + 1):
            v = tbuf[(g, h % 3, 0) + cut(q)]
            for d in range(2):
                v += come(g, h - 1, q, d)
            r, c = cut(q)
            fg_ref[r, g * gw + c.start:g * gw + c.stop] = v.astype(BF)

    weight_terms()
    order = []
    for g in range(G):
        for a in range(2):
            grad_forward(g, a)
            grad_ready(g, a)
            for s in range(2):
                ring_unit(g, s, 2 * a + s)
                order.append((g, s, 2 * a + s))
        if g == 0:
            side.pop()()
    n = 0
    while n < len(order):
        g, s, u = order[n]
        if s + 1 < h:
            ring_unit(g, s + 1, u)
            order.append((g, s + 1, u))
        elif all((g, s, u - u % 2 + k) in order[:n + 1] for k in range(2)):
            ring_end(g, u // 2)
        n += 1
        if n in SIDE_AT and len(side) > 1:
            side.pop()()
    while side:
        side.pop()()

    for c in sent:
        c.wait_send()
    for c in pending.values():
        c.wait_send()


def finish_kernel(scale, act_in, wsum_in, fg_in, act_out, wg_out, fg_out, wide, sems):
    copies = [
        pltpu.make_async_copy(act_in, act_out, sems.at[0]),
        pltpu.make_async_copy(fg_in, fg_out, sems.at[1]),
    ]
    for c in copies:
        c.start()
    R, wr, F = wsum_in.shape
    for k in range(R):
        at = slice(k * wr, (k + 1) * wr)
        wide[at, :] = wsum_in[k].astype(F32) * scale
        c = pltpu.make_async_copy(wide.at[at, :], wg_out.at[at, :], sems.at[2 + k])
        c.start()
        copies.append(c)
    for c in copies:
        c.wait()


def local(N, R, features, weight, cotangent, tile_values, tile_row, tile_col, tile_count):
    rows, F = features.shape
    cap = tile_values.shape[0]
    subs = rows // TB
    blocks = subs * R
    G, T, Q = 2, 4, 4
    gw, h, M = F // G, N // 2, R // 2
    D = min(h, 4)
    wr = F // R
    Z, hx = N // 2, wr // 2
    pa = min(Z, hx // 16)
    ph, pw = hx // pa, F // (Z // pa)
    places = N * blocks * subs
    has_t = N * rows * rows * R * 2 <= 8 * 1024 * 1024
    cfg = (N, R, G, D, T, cap, blocks, subs, has_t)
    dma = pltpu.SemaphoreType.DMA
    V = pltpu.VMEM
    M1 = max(M - 1, 1)
    scratch = [
        V((1, cap), jnp.int32), V((1, cap), jnp.int32),
        V((cap, TB, TB), BF), V((cap + 1, TB, TB), BF),
        V((R * rows, N * rows), BF),
        V((N * rows, R * rows) if has_t else (16, TB), BF),
        V((G, N * rows, gw), BF), V((G, R, rows, gw), F32),
        V((G, M, rows, gw), BF), V((G, M, rows, gw), BF), V((G, M1, rows, gw), BF), V((G, M1, rows, gw), BF),
        V((rows, F), BF), V((rows, F), F32), V((rows, F), BF), V((F, F), BF), V((F, F), BF), V((rows, F), BF),
        V((G, R, rows, gw), BF), V((G, D, 2, rows, gw), BF), V((G, h, 2, rows, gw), BF),
        V((G, 3, 2, rows, gw), F32), V((F, rows), BF),
        V((R, wr, F), F32), V((R, wr, F), BF), V((M, wr, F), BF),
        V((M1, wr, F), BF), V((M1, wr, F), BF),
        V((hx, F), BF), V((hx, F), BF), V((hx, F), BF), V((Z - 1, ph, pw), BF), V((R, wr, F), BF),
        V((1, cap), jnp.int32), V((1, places), jnp.int32),
        pltpu.SMEM((1, cap), jnp.int32), pltpu.SMEM((1, places), jnp.int32),
        dma((G + 2,)), dma((T,)), dma((4,)), dma((G, h, Q, 2)), dma((G, h, Q, 2)),
        dma((G, 2, M)), dma((G, 2, M)), dma((G, 2, M1)), dma((G, 2, M1)),
        dma((G, 2, M)), dma((G, 2, M)), dma((G, 2, M1)), dma((G, 2, M1)),
        dma((G, h, Q, 2)), dma((G, h, Q, 2)),
        dma((M,)), dma((M,)), dma((M,)), dma((M,)), dma((2,)),
        dma((Z - 1,)), dma((Z - 1,)), dma((N - 1,)), dma((N - 1,)),
        dma((M,)), dma((M,)), dma((M,)), dma((M,)),
    ]
    smem = pl.BlockSpec(memory_space=pltpu.SMEM)
    vmem = pl.BlockSpec(memory_space=pltpu.VMEM)
    hbm = pl.BlockSpec(memory_space=pltpu.HBM)
    act, wsum, feature_grad = pl.pallas_call(
        functools.partial(layer_kernel, cfg),
        out_shape=(
            jax.ShapeDtypeStruct((rows, F), BF),
            jax.ShapeDtypeStruct((R, wr, F), BF),
            jax.ShapeDtypeStruct((rows, F), BF),
        ),
        in_specs=[smem] + [hbm] * 6,
        out_specs=(vmem, vmem, vmem),
        scratch_shapes=scratch,
        compiler_params=pltpu.CompilerParams(
            collective_id=0, has_side_effects=True,
            vmem_limit_bytes=(48 if has_t else 63) * 1024 * 1024,
        ),
        name="layer",
    )(
        tile_count,
        *(
            pltpu.with_memory_space_constraint(v, pltpu.HBM)
            for v in (
                tile_row.reshape(1, cap), tile_col.reshape(1, cap),
                features, weight, cotangent, tile_values,
            )
        ),
    )
    scale = 1.0 / math.sqrt(rows * R * N)
    act, weight_grad, feature_grad = pl.pallas_call(
        functools.partial(finish_kernel, scale),
        out_shape=(
            jax.ShapeDtypeStruct((rows, F), BF),
            jax.ShapeDtypeStruct((F, F), F32),
            jax.ShapeDtypeStruct((rows, F), BF),
        ),
        in_specs=[vmem, vmem, vmem],
        out_specs=(hbm, hbm, hbm),
        scratch_shapes=[V((F, F), F32), dma((2 + R,))],
        compiler_params=pltpu.CompilerParams(vmem_limit_bytes=8 * 1024 * 1024),
        name="finish",
    )(act, wsum, feature_grad)
    return act, weight_grad, feature_grad


def solution(mesh):
    in_specs = (
        P(("node", "rep"), None),
        P(),
        P(("node", "rep"), None),
        P(("node", "rep"), None, None),
        P(("node", "rep")),
        P(("node", "rep")),
        P(("node", "rep")),
    )
    out_specs = (P(("node", "rep"), None), P(), P(("node", "rep"), None))
    step = functools.partial(local, mesh.shape["node"], mesh.shape["rep"])
    return jax.shard_map(step, mesh=mesh, in_specs=in_specs, out_specs=out_specs, check_vma=False)
```

```python
import functools
import math

import jax
import jax.numpy as jnp
from jax import lax
from jax.experimental import pallas as pl
from jax.experimental.pallas import tpu as pltpu
from jax.sharding import PartitionSpec as P

TB = 128
FIRST = 4
SIDE_AT = (1, 5, 9, 17, 23)
MESH = pl.DeviceIdType.MESH
BF = jnp.bfloat16
F32 = jnp.float32


def mm(a, b):
    return jnp.dot(a, b, preferred_element_type=F32)


def layer_kernel(
    cfg, count_ref, row_hbm, col_hbm, x_hbm, w_hbm, c_hbm, tiles_hbm,
    act_ref, wsum_ref, fg_ref,
    row_ref, col_ref, tiles, stage, dense, dense_t, X, part, psend, p1, p2s, p2, agg, pre, pg, w_ref, wt, c_ref,
    rg, rsb, rrb, tbuf, aggt, wterm, wsend, wa, wb, wbs, wxs, wx, wq, wc, wfull,
    key_v, last_v, key_ref, last_ref,
    in_sem, tile_sem, plan_sem, gs, gr, p1s, p1r, p2ss, p2r, as_, ar, fs, fr, rs, rr,
    was, war, wbss, wbr, wxsem, wcs, wcr, wds, wdr, wes, wer, wfs, wfr,
):
    N, R, G, D, T, cap, blocks, subs, has_t = cfg
    h, M = N // 2, R // 2
    rows, F = act_ref.shape
    gw = F // G
    hr, hw = rows // 2, gw // 2
    Q = 4
    i = lax.axis_index("node")
    j = lax.axis_index("rep")
    mine, par = lax.div(j, 2), lax.rem(j, 2)
    partner = (i, j + 1 - 2 * par)
    z, x = lax.div(i, 2), lax.rem(i, 2)
    pos = z + x * (N - 1 - 2 * z)

    def node_at(k):
        p = lax.rem(pos + (k + N), N)
        xx = lax.div(p, N // 2)
        return 2 * (p + xx * (N - 1 - 2 * p)) + xx

    right, left = node_at(1), node_at(-1)
    ring_to = (right, left)
    sent = []

    def rcopy(src, dst, ssem, rsem, dev):
        return pltpu.make_async_remote_copy(
            src_ref=src, dst_ref=dst, send_sem=ssem, recv_sem=rsem,
            device_id=dev, device_id_type=MESH,
        )

    def send(src, dst, ssem, rsem, dev):
        c = rcopy(src, dst, ssem, rsem, dev)
        c.start()
        sent.append(c)

    def arrived(dst, ssem, rsem):
        rcopy(dst, dst, ssem, rsem, (i, j)).wait_recv()

    def peer(k):
        return 2 * lax.rem(mine + k + M, M) + par

    def block(o):
        return pl.ds(pl.multiple_of(o * rows, rows), rows)

    def lanes(a):
        return pl.ds(a * hw, hw)

    def unit(q):
        return pl.ds(q % 2 * hr, hr), lanes(q // 2)

    def unit_of(o, q):
        return pl.ds(pl.multiple_of(o * rows + q % 2 * hr, hr), hr), lanes(q // 2)

    ins = [
        pltpu.make_async_copy(x_hbm.at[:, pl.ds(g * gw, gw)], X.at[g, block(i), :], in_sem.at[g])
        for g in range(G)
    ]
    ins.append(pltpu.make_async_copy(w_hbm, w_ref, in_sem.at[G]))
    ins.append(pltpu.make_async_copy(c_hbm, c_ref, in_sem.at[G + 1]))
    per = cap // T
    tile_copies = [
        pltpu.make_async_copy(
            tiles_hbm.at[pl.ds(k * per, per)], tiles.at[pl.ds(k * per, per)], tile_sem.at[k]
        )
        for k in range(T)
    ]
    spots = [
        pltpu.make_async_copy(row_hbm, row_ref, plan_sem.at[2]),
        pltpu.make_async_copy(col_hbm, col_ref, plan_sem.at[3]),
    ]
    for c in spots + ins + tile_copies:
        c.start()

    barrier = pltpu.get_barrier_semaphore()
    for n in ring_to:
        pl.semaphore_signal(barrier, inc=1, device_id=(n, j), device_id_type=MESH)
    for k in range(1, R):
        pl.semaphore_signal(barrier, inc=1, device_id=(i, lax.rem(j + k, R)), device_id_type=MESH)

    for g in range(G):
        ins[g].wait()
    pl.semaphore_wait(barrier, 2 + R - 1)

    def gather_send(g, s, q, d):
        at = (g,) + unit_of(node_at(-s if d == 0 else s), q)
        send(X.at[at], X.at[at], gs.at[g, s, q, d], gr.at[g, s, q, d], (ring_to[d], j))

    order, late = [(0, 0, q) for q in range(Q)], [(g, 0, q) for g in range(1, G) for q in range(Q)]
    order, late = order + late[:FIRST], late[FIRST:]
    first, events, n = list(order), [], 0
    while n < len(order):
        g, s, q = order[n]
        out = []
        if s + 1 < h - 1 or (s + 1 == h - 1 and q % 2 == 0):
            out.append((g, s + 1, q))
        if late and n >= 2:
            out.append(late.pop(0))
        order += out
        events.append(((g, s, q), out))
        n += 1
    events.reverse()

    def flip(q, d):
        return q - q % 2 + (q + d) % 2

    def event(count=1):
        for _ in range(min(count, len(events))):
            (g, s, q), out = events.pop()
            for d in range(2):
                at = (g,) + unit_of(node_at(-(s + 1) if d == 0 else s + 1), flip(q, d))
                arrived(X.at[at], gs.at[g, s, flip(q, d), d], gr.at[g, s, flip(q, d), d])
                for to in out:
                    gather_send(to[0], to[1], flip(to[2], d), d)

    def need(g, s, a):
        while any(e[0][0] == g and e[0][1] <= s and e[0][2] // 2 in a for e in events):
            event()

    for g, s, q in first:
        for d in range(2):
            gather_send(g, s, flip(q, d), d)

    for c in spots:
        c.wait()
    places = N * blocks * subs
    slot_row = lax.broadcasted_iota(jnp.int32, (1, cap), 1)
    col = col_ref[...]
    place_row = (lax.div(col, subs) * blocks + row_ref[...]) * subs + lax.rem(col, subs)
    place_row = jnp.where(slot_row < count_ref[0], place_row, places)
    key_row = (place_row * cap + slot_row).astype(F32)
    down = lax.broadcasted_iota(jnp.int32, (cap, cap), 0)
    across = lax.broadcasted_iota(jnp.int32, (cap, cap), 1)
    keys = jnp.broadcast_to(key_row, (cap, cap))
    place_all = jnp.broadcast_to(place_row.astype(F32), (cap, cap))
    key_col = jnp.sum(jnp.where(down == across, keys, 0.0), axis=1, keepdims=True)
    place_col = jnp.sum(jnp.where(down == across, place_all, 0.0), axis=1, keepdims=True)
    rank = jnp.sum(jnp.where(keys < key_col, 1.0, 0.0), axis=1, keepdims=True)
    key_v[...] = jnp.sum(
        jnp.where(rank == across.astype(F32), key_col, 0.0), axis=0, keepdims=True
    ).astype(jnp.int32)
    spot = lax.broadcasted_iota(jnp.int32, (cap, places), 1).astype(F32)
    upto = jnp.sum(jnp.where(place_col <= spot, 1.0, 0.0), axis=0, keepdims=True)
    there = jnp.sum(jnp.where(place_col == spot, 1.0, 0.0), axis=0, keepdims=True)
    last_v[...] = jnp.where(there > 0.0, upto - 1.0, float(cap)).astype(jnp.int32)
    plan = [
        pltpu.make_async_copy(key_v, key_ref, plan_sem.at[0]),
        pltpu.make_async_copy(last_v, last_ref, plan_sem.at[1]),
    ]
    for c in plan:
        c.start()
    for c in ins[G:] + tile_copies + plan:
        c.wait()
    wt[...] = w_ref[...].T
    stage[cap] = jnp.zeros((TB, TB), BF)

    def slot_step(p, carry):
        acc, prev = carry
        key = jnp.maximum(key_ref[0, p], 0)
        slot = lax.rem(key, cap)
        place = lax.div(key, cap)
        keep = jnp.where(place == prev, 1.0, 0.0).astype(F32)
        acc = acc * keep + tiles[slot].astype(F32)
        stage[p] = acc.astype(BF)
        return acc, place

    carry = (jnp.zeros((TB, TB), F32), jnp.int32(-1))
    for k in range(4):
        carry = lax.fori_loop(cap * k // 4, cap * (k + 1) // 4, slot_step, carry)
        event()

    def place_step(o, carry):
        for r in range(blocks):
            for s in range(subs):
                tile = stage[jnp.clip(last_ref[0, (o * blocks + r) * subs + s], 0, cap)]
                at = pl.ds(pl.multiple_of((o * subs + s) * TB, TB), TB)
                dense[r * TB:(r + 1) * TB, at] = tile
                if has_t:
                    dense_t[at, r * TB:(r + 1) * TB] = tile.T
        return carry

    for k in range(2):
        lax.fori_loop(N * k // 2, N * (k + 1) // 2, place_step, 0)
        event()

    def chip_send(g, a, m, value):
        psend[g, m, :, a * hw:(a + 1) * hw] = value.astype(BF)
        at = (g, m, slice(None), lanes(a))
        send(psend.at[at], p1.at[at], p1s.at[g, a, m], p1r.at[g, a, m], partner)

    def chip_sum(g, a):
        at = slice(a * hw, (a + 1) * hw)
        for k in range(M - 1, -1, -1):
            m = lax.rem(mine + k, M)
            spot = p1.at[g, m, :, lanes(a)]
            arrived(spot, p1s.at[g, a, m], p1r.at[g, a, m])
            total = part[g, 2 * m + par, :, at] + p1[g, m, :, at].astype(F32)
            if k:
                p2s[g, k - 1, :, at] = total.astype(BF)
                spot = (g, k - 1, slice(None), lanes(a))
                send(p2s.at[spot], p2.at[spot], p2ss.at[g, a, k - 1], p2r.at[g, a, k - 1], (i, peer(k)))
            else:
                part[g, j, :, at] = total

    def rep_sum(g, a):
        at = slice(a * hw, (a + 1) * hw)
        total = part[g, j, :, at]
        for k in range(1, M):
            arrived(p2.at[g, k - 1, :, lanes(a)], p2ss.at[g, a, k - 1], p2r.at[g, a, k - 1])
            total += p2[g, k - 1, :, at].astype(F32)
        cols = slice(g * gw + a * hw, g * gw + (a + 1) * hw)
        agg[:, cols] = total.astype(BF)
        t = mm(agg[:, cols], w_ref[cols, :])
        pre[...] = t if g == 0 and a == 0 else pre[...] + t

    def block_part(g, offsets, first):
        def one(m, carry):
            total = None if first else part[g, m]
            for k in offsets:
                cols = block(node_at(k))
                t = mm(dense[block(m), cols], X[g, cols, :])
                total = t if total is None else total + t
            part[g, m] = total
            return carry

        lax.fori_loop(0, R, one, 0)

    def last_block(g, a):
        cols = block(node_at(h))
        at = slice(a * hw, (a + 1) * hw)
        need(g, h - 1, (a,))
        for k in range(M - 1, -1, -1):
            m = lax.rem(mine + k, M)
            jj = 2 * m + 1 - par
            chip_send(g, a, m, part[g, jj, :, at] + mm(dense[block(jj), cols], X[g, cols, at]))
        for m in range(M):
            jj = 2 * m + par
            part[g, jj, :, at] = part[g, jj, :, at] + mm(dense[block(jj), cols], X[g, cols, at])

    for g in range(G):
        block_part(g, [0], True)
        event()
    for s in range(h - 1):
        for g in range(G):
            need(g, s, (0, 1))
            block_part(g, [-(s + 1), s + 1], False)
    halves = [(g, a) for g in range(G) for a in range(2)]
    for k, (g, a) in enumerate(halves):
        last_block(g, a)
        if k == len(halves) - 2:
            for done in halves[:-1]:
                chip_sum(*done)
    for done in halves[-1:]:
        chip_sum(*done)
    for done in halves:
        rep_sum(*done)

    root = math.sqrt(2.0 / math.pi)
    step = 64 if rows % 64 == 0 else rows

    def act_step(b, carry):
        at = pl.ds(pl.multiple_of(b * step, step), step)
        v = pre[at, :]
        v2 = v * v
        t = jnp.tanh(root * (v + 0.044715 * (v2 * v)))
        half_up = 0.5 * (1.0 + t)
        act_ref[at, :] = (v * half_up).astype(BF)
        slope = half_up + (0.5 * v) * (1.0 - t * t) * (root * (1.0 + (3 * 0.044715) * v2))
        pg[at, :] = (c_ref[at, :].astype(F32) * slope).astype(BF)
        return carry

    lax.fori_loop(0, rows // step, act_step, 0)

    def grad_at(g, jj, a):
        return rg.at[g, jj, :, lanes(a)]

    for g in range(G):
        for a in range(2):
            cols = slice(g * gw + a * hw, g * gw + (a + 1) * hw)
            rg[g, j, :, a * hw:(a + 1) * hw] = mm(pg[...], wt[:, cols]).astype(BF)
            spot = grad_at(g, j, a)
            for k in range(1, M):
                send(spot, spot, as_.at[g, a, k], ar.at[g, a, k], (i, peer(k)))
            send(spot, spot, as_.at[g, a, 0], ar.at[g, a, 0], partner)

    def grad_forward(g, a):
        for k in range(1, M):
            spot = grad_at(g, peer(-k), a)
            arrived(spot, as_.at[g, a, k], ar.at[g, a, k])
            send(spot, spot, fs.at[g, a, k - 1], fr.at[g, a, k - 1], partner)

    def grad_ready(g, a):
        arrived(grad_at(g, j + 1 - 2 * par, a), as_.at[g, a, 0], ar.at[g, a, 0])
        for k in range(1, M):
            spot = grad_at(g, peer(-k) + 1 - 2 * par, a)
            arrived(spot, fs.at[g, a, k - 1], fr.at[g, a, k - 1])

    wr = F // R
    Z, hx = N // 2, wr // 2
    pa = min(Z, hx // 16)
    pb = Z // pa
    ph, pw = hx // pa, F // pb

    def weight_terms():
        aggt[...] = agg[...].T

        def one(k, carry):
            at = pl.ds(pl.multiple_of(k * wr, wr), wr)
            t = mm(aggt[at, :], pg[...])
            wterm[k] = t
            wsend[k] = t.astype(BF)
            return carry

        lax.fori_loop(0, R, one, 0)
        for m in range(M):
            send(wsend.at[2 * m + 1 - par], wa.at[m], was.at[m], war.at[m], partner)

    def weight_chip():
        for m in range(M):
            arrived(wa.at[m], was.at[m], war.at[m])
            wterm[2 * m + par] = wterm[2 * m + par] + wa[m].astype(F32)
        for k in range(1, M):
            to = lax.rem(mine + k, M)
            wbs[k - 1] = wterm[2 * to + par].astype(BF)
            send(wbs.at[k - 1], wb.at[k - 1], wbss.at[k - 1], wbr.at[k - 1], (i, 2 * to + par))

    across_node = (i + 1 - 2 * x, j)

    def half_rows(b):
        return pl.ds(pl.multiple_of(b * hx, hx), hx)

    def other(k):
        return lax.rem(z + k + Z, Z)

    def piece(n, base):
        return (
            pl.ds(pl.multiple_of(base + lax.div(n, pb) * ph, ph), ph),
            pl.ds(pl.multiple_of(lax.rem(n, pb) * pw, pw), pw),
        )

    def weight_rep():
        for b in (1 - x, x):
            total = wterm[j, half_rows(b), :]
            for k in range(1, M):
                if b is not x:
                    arrived(wb.at[k - 1], wbss.at[k - 1], wbr.at[k - 1])
                total += wb[k - 1, half_rows(b), :].astype(F32)
            if b is x:
                wterm[j, half_rows(b), :] = total
            else:
                wxs[...] = total.astype(BF)
                send(wxs, wx, wxsem.at[0], wxsem.at[1], across_node)

    def weight_pair():
        arrived(wx, wxsem.at[0], wxsem.at[1])
        wq[...] = (wterm[j, half_rows(x), :] + wx[...].astype(F32)).astype(BF)
        for k in range(1, Z):
            n = other(k)
            send(wq.at[piece(n, 0)], wc.at[k - 1], wcs.at[k - 1], wcr.at[k - 1], (2 * n + x, j))

    def weight_node():
        total = wq[piece(z, 0)].astype(F32)
        for k in range(1, Z):
            arrived(wc.at[k - 1], wcs.at[k - 1], wcr.at[k - 1])
            total += wc[k - 1].astype(F32)
        at = (j,) + piece(z, x * hx)
        wfull[at] = total.astype(BF)
        for k in range(1, N):
            send(wfull.at[at], wfull.at[at], wds.at[k - 1], wdr.at[k - 1], (lax.rem(i + k, N), j))

    def weight_spread():
        for k in range(1, N):
            n = lax.rem(i - k + N, N)
            at = (j,) + piece(lax.div(n, 2), lax.rem(n, 2) * hx)
            arrived(wfull.at[at], wds.at[k - 1], wdr.at[k - 1])
        spot = wfull.at[j]
        for k in range(1, M):
            send(spot, spot, wes.at[k], wer.at[k], (i, peer(k)))
        send(spot, spot, wes.at[0], wer.at[0], partner)

    def weight_forward():
        for k in range(1, M):
            spot = wfull.at[peer(-k)]
            arrived(spot, wes.at[k], wer.at[k])
            send(spot, spot, wfs.at[k - 1], wfr.at[k - 1], partner)

    def weight_end():
        arrived(wfull.at[j + 1 - 2 * par], wes.at[0], wer.at[0])
        for k in range(1, M):
            spot = wfull.at[peer(-k) + 1 - 2 * par]
            arrived(spot, wfs.at[k - 1], wfr.at[k - 1])
        wsum_ref[...] = wfull[...]

    side = [
        weight_end, weight_forward, weight_spread,
        weight_node, weight_pair, weight_rep, weight_chip,
    ]

    def term(g, o, at):
        grads = rg[g, :, :, at]
        grads = grads.reshape(R * rows, grads.shape[-1])
        if has_t:
            return mm(dense_t[block(o), :], grads)
        return lax.dot_general(
            dense[:, block(o)], grads, (((0,), (0,)), ((), ())), preferred_element_type=F32
        )

    pending = {}

    def ring_send(g, s, q, d):
        at = unit(q)
        c = rcopy(
            rsb.at[(g, s % D, d) + at], rrb.at[(g, s, d) + at],
            rs.at[g, s, q, d], rr.at[g, s, q, d], (ring_to[d], j),
        )
        c.start()
        pending[(g, s, q, d)] = c

    def cut(q):
        return slice(q % 2 * hr, (q % 2 + 1) * hr), slice(q // 2 * hw, (q // 2 + 1) * hw)

    made = set()

    def make(g, s, a):
        key = (g, s, a if s < 2 else 0)
        if key in made:
            return
        made.add(key)
        at = slice(a * hw, (a + 1) * hw) if s < 2 else slice(None)
        if s == 0 or s == h:
            tbuf[g, s % 3, 0, :, at] = term(g, node_at(h) if s == 0 else i, at)
        else:
            for d in range(2):
                tbuf[g, s % 3, d, :, at] = term(g, node_at(h - s if d == 0 else s - h), at)

    def come(g, s, q, d):
        arrived(rrb.at[(g, s, d) + unit(q)], rs.at[g, s, q, d], rr.at[g, s, q, d])
        return rrb[(g, s, d) + cut(q)].astype(F32)

    def ring_unit(g, s, u):
        make(g, s, u // 2)
        for d in range(2):
            q = flip(u, d)
            v = tbuf[(g, s % 3, d if s else 0) + cut(q)]
            if s > 1 or (s == 1 and u % 2 == 0):
                v += come(g, s - 1, q, d)
            if (g, s - D, q, d) in pending:
                pending.pop((g, s - D, q, d)).wait_send()
            rsb[(g, s % D, d) + cut(q)] = v.astype(BF)
            ring_send(g, s, q, d)

    def ring_end(g, a):
        make(g, h, a)
        for q in (2 * a, 2 * a + 1):
            v = tbuf[(g, h % 3, 0) + cut(q)]
            for d in range(2):
                v += come(g, h - 1, q, d)
            r, c = cut(q)
            fg_ref[r, g * gw + c.start:g * gw + c.stop] = v.astype(BF)

    weight_terms()
    side.pop()()
    order = []
    for g in range(G):
        for a in range(2):
            grad_forward(g, a)
            grad_ready(g, a)
            for s in range(2):
                ring_unit(g, s, 2 * a + s)
                order.append((g, s, 2 * a + s))
    n = 0
    while n < len(order):
        g, s, u = order[n]
        if s + 1 < h:
            ring_unit(g, s + 1, u)
            order.append((g, s + 1, u))
        elif all((g, s, u - u % 2 + k) in order[:n + 1] for k in range(2)):
            ring_end(g, u // 2)
        n += 1
        if n in SIDE_AT and len(side) > 1:
            side.pop()()
    while side:
        side.pop()()

    for c in sent:
        c.wait_send()
    for c in pending.values():
        c.wait_send()


def finish_kernel(scale, act_in, wsum_in, fg_in, act_out, wg_out, fg_out, wide, sems):
    copies = [
        pltpu.make_async_copy(act_in, act_out, sems.at[0]),
        pltpu.make_async_copy(fg_in, fg_out, sems.at[1]),
    ]
    for c in copies:
        c.start()
    R, wr, F = wsum_in.shape
    for k in range(R):
        at = slice(k * wr, (k + 1) * wr)
        wide[at, :] = wsum_in[k].astype(F32) * scale
        c = pltpu.make_async_copy(wide.at[at, :], wg_out.at[at, :], sems.at[2 + k])
        c.start()
        copies.append(c)
    for c in copies:
        c.wait()


def local(N, R, features, weight, cotangent, tile_values, tile_row, tile_col, tile_count):
    rows, F = features.shape
    cap = tile_values.shape[0]
    subs = rows // TB
    blocks = subs * R
    G, T, Q = 2, 4, 4
    gw, h, M = F // G, N // 2, R // 2
    D = min(h, 4)
    wr = F // R
    Z, hx = N // 2, wr // 2
    pa = min(Z, hx // 16)
    ph, pw = hx // pa, F // (Z // pa)
    places = N * blocks * subs
    has_t = N * rows * rows * R * 2 <= 8 * 1024 * 1024
    cfg = (N, R, G, D, T, cap, blocks, subs, has_t)
    dma = pltpu.SemaphoreType.DMA
    V = pltpu.VMEM
    M1 = max(M - 1, 1)
    scratch = [
        V((1, cap), jnp.int32), V((1, cap), jnp.int32),
        V((cap, TB, TB), BF), V((cap + 1, TB, TB), BF),
        V((R * rows, N * rows), BF),
        V((N * rows, R * rows) if has_t else (16, TB), BF),
        V((G, N * rows, gw), BF), V((G, R, rows, gw), F32),
        V((G, M, rows, gw), BF), V((G, M, rows, gw), BF), V((G, M1, rows, gw), BF), V((G, M1, rows, gw), BF),
        V((rows, F), BF), V((rows, F), F32), V((rows, F), BF), V((F, F), BF), V((F, F), BF), V((rows, F), BF),
        V((G, R, rows, gw), BF), V((G, D, 2, rows, gw), BF), V((G, h, 2, rows, gw), BF),
        V((G, 3, 2, rows, gw), F32), V((F, rows), BF),
        V((R, wr, F), F32), V((R, wr, F), BF), V((M, wr, F), BF),
        V((M1, wr, F), BF), V((M1, wr, F), BF),
        V((hx, F), BF), V((hx, F), BF), V((hx, F), BF), V((Z - 1, ph, pw), BF), V((R, wr, F), BF),
        V((1, cap), jnp.int32), V((1, places), jnp.int32),
        pltpu.SMEM((1, cap), jnp.int32), pltpu.SMEM((1, places), jnp.int32),
        dma((G + 2,)), dma((T,)), dma((4,)), dma((G, h, Q, 2)), dma((G, h, Q, 2)),
        dma((G, 2, M)), dma((G, 2, M)), dma((G, 2, M1)), dma((G, 2, M1)),
        dma((G, 2, M)), dma((G, 2, M)), dma((G, 2, M1)), dma((G, 2, M1)),
        dma((G, h, Q, 2)), dma((G, h, Q, 2)),
        dma((M,)), dma((M,)), dma((M,)), dma((M,)), dma((2,)),
        dma((Z - 1,)), dma((Z - 1,)), dma((N - 1,)), dma((N - 1,)),
        dma((M,)), dma((M,)), dma((M,)), dma((M,)),
    ]
    smem = pl.BlockSpec(memory_space=pltpu.SMEM)
    vmem = pl.BlockSpec(memory_space=pltpu.VMEM)
    hbm = pl.BlockSpec(memory_space=pltpu.HBM)
    act, wsum, feature_grad = pl.pallas_call(
        functools.partial(layer_kernel, cfg),
        out_shape=(
            jax.ShapeDtypeStruct((rows, F), BF),
            jax.ShapeDtypeStruct((R, wr, F), BF),
            jax.ShapeDtypeStruct((rows, F), BF),
        ),
        in_specs=[smem] + [hbm] * 6,
        out_specs=(vmem, vmem, vmem),
        scratch_shapes=scratch,
        compiler_params=pltpu.CompilerParams(
            collective_id=0, has_side_effects=True,
            vmem_limit_bytes=(48 if has_t else 63) * 1024 * 1024,
        ),
        name="layer",
    )(
        tile_count,
        *(
            pltpu.with_memory_space_constraint(v, pltpu.HBM)
            for v in (
                tile_row.reshape(1, cap), tile_col.reshape(1, cap),
                features, weight, cotangent, tile_values,
            )
        ),
    )
    scale = 1.0 / math.sqrt(rows * R * N)
    act, weight_grad, feature_grad = pl.pallas_call(
        functools.partial(finish_kernel, scale),
        out_shape=(
            jax.ShapeDtypeStruct((rows, F), BF),
            jax.ShapeDtypeStruct((F, F), F32),
            jax.ShapeDtypeStruct((rows, F), BF),
        ),
        in_specs=[vmem, vmem, vmem],
        out_specs=(hbm, hbm, hbm),
        scratch_shapes=[V((F, F), F32), dma((2 + R,))],
        compiler_params=pltpu.CompilerParams(vmem_limit_bytes=8 * 1024 * 1024),
        name="finish",
    )(act, wsum, feature_grad)
    return act, weight_grad, feature_grad


def solution(mesh):
    in_specs = (
        P(("node", "rep"), None),
        P(),
        P(("node", "rep"), None),
        P(("node", "rep"), None, None),
        P(("node", "rep")),
        P(("node", "rep")),
        P(("node", "rep")),
    )
    out_specs = (P(("node", "rep"), None), P(), P(("node", "rep"), None))
    step = functools.partial(local, mesh.shape["node"], mesh.shape["rep"])
    return jax.shard_map(step, mesh=mesh, in_specs=in_specs, out_specs=out_specs, check_vma=False)
```

```python
import functools
import math

import jax
import jax.numpy as jnp
from jax import lax
from jax.experimental import pallas as pl
from jax.experimental.pallas import tpu as pltpu
from jax.sharding import PartitionSpec as P

TB = 128
FIRST = 4
SIDE_AT = (2, 6, 11, 20, 26)
MESH = pl.DeviceIdType.MESH
BF = jnp.bfloat16
F32 = jnp.float32


def mm(a, b):
    return jnp.dot(a, b, preferred_element_type=F32)


def layer_kernel(
    cfg, count_ref, row_hbm, col_hbm, x_hbm, w_hbm, c_hbm, tiles_hbm,
    act_ref, wsum_ref, fg_ref,
    row_ref, col_ref, tiles, stage, dense, dense_t, X, part, psend, p1, p2s, p2, agg, pre, pg, w_ref, wt, c_ref,
    rg, rsb, rrb, tbuf, aggt, wterm, wsend, wa, wb, wbs, wxs, wx, wq, wc, wfull,
    key_v, last_v, key_ref, last_ref,
    in_sem, tile_sem, plan_sem, gs, gr, p1s, p1r, p2ss, p2r, as_, ar, fs, fr, rs, rr,
    was, war, wbss, wbr, wxsem, wcs, wcr, wds, wdr, wes, wer, wfs, wfr,
):
    N, R, G, D, T, cap, blocks, subs, has_t = cfg
    h, M = N // 2, R // 2
    rows, F = act_ref.shape
    gw = F // G
    hr, hw = rows // 2, gw // 2
    Q = 4
    i = lax.axis_index("node")
    j = lax.axis_index("rep")
    mine, par = lax.div(j, 2), lax.rem(j, 2)
    partner = (i, j + 1 - 2 * par)
    z, x = lax.div(i, 2), lax.rem(i, 2)
    pos = z + x * (N - 1 - 2 * z)

    def node_at(k):
        p = lax.rem(pos + (k + N), N)
        xx = lax.div(p, N // 2)
        return 2 * (p + xx * (N - 1 - 2 * p)) + xx

    right, left = node_at(1), node_at(-1)
    ring_to = (right, left)
    sent = []

    def rcopy(src, dst, ssem, rsem, dev):
        return pltpu.make_async_remote_copy(
            src_ref=src, dst_ref=dst, send_sem=ssem, recv_sem=rsem,
            device_id=dev, device_id_type=MESH,
        )

    def send(src, dst, ssem, rsem, dev):
        c = rcopy(src, dst, ssem, rsem, dev)
        c.start()
        sent.append(c)

    def arrived(dst, ssem, rsem):
        rcopy(dst, dst, ssem, rsem, (i, j)).wait_recv()

    def peer(k):
        return 2 * lax.rem(mine + k + M, M) + par

    def block(o):
        return pl.ds(pl.multiple_of(o * rows, rows), rows)

    def lanes(a):
        return pl.ds(a * hw, hw)

    def unit(q):
        return pl.ds(q % 2 * hr, hr), lanes(q // 2)

    def unit_of(o, q):
        return pl.ds(pl.multiple_of(o * rows + q % 2 * hr, hr), hr), lanes(q // 2)

    ins = [
        pltpu.make_async_copy(x_hbm.at[:, pl.ds(g * gw, gw)], X.at[g, block(i), :], in_sem.at[g])
        for g in range(G)
    ]
    ins.append(pltpu.make_async_copy(w_hbm, w_ref, in_sem.at[G]))
    ins.append(pltpu.make_async_copy(c_hbm, c_ref, in_sem.at[G + 1]))
    per = cap // T
    tile_copies = [
        pltpu.make_async_copy(
            tiles_hbm.at[pl.ds(k * per, per)], tiles.at[pl.ds(k * per, per)], tile_sem.at[k]
        )
        for k in range(T)
    ]
    spots = [
        pltpu.make_async_copy(row_hbm, row_ref, plan_sem.at[2]),
        pltpu.make_async_copy(col_hbm, col_ref, plan_sem.at[3]),
    ]
    for c in spots + ins + tile_copies:
        c.start()

    barrier = pltpu.get_barrier_semaphore()
    for n in ring_to:
        pl.semaphore_signal(barrier, inc=1, device_id=(n, j), device_id_type=MESH)
    for k in range(1, R):
        pl.semaphore_signal(barrier, inc=1, device_id=(i, lax.rem(j + k, R)), device_id_type=MESH)

    for g in range(G):
        ins[g].wait()
    pl.semaphore_wait(barrier, 2 + R - 1)

    def gather_send(g, s, q, d):
        at = (g,) + unit_of(node_at(-s if d == 0 else s), q)
        send(X.at[at], X.at[at], gs.at[g, s, q, d], gr.at[g, s, q, d], (ring_to[d], j))

    order, late = [(0, 0, q) for q in range(Q)], [(g, 0, q) for g in range(1, G) for q in range(Q)]
    order, late = order + late[:FIRST], late[FIRST:]
    first, events, n = list(order), [], 0
    while n < len(order):
        g, s, q = order[n]
        out = []
        if s + 1 < h - 1 or (s + 1 == h - 1 and q % 2 == 0):
            out.append((g, s + 1, q))
        if late and n >= 2:
            out.append(late.pop(0))
        order += out
        events.append(((g, s, q), out))
        n += 1
    events.reverse()

    def flip(q, d):
        return q - q % 2 + (q + d) % 2

    def event(count=1):
        for _ in range(min(count, len(events))):
            (g, s, q), out = events.pop()
            for d in range(2):
                at = (g,) + unit_of(node_at(-(s + 1) if d == 0 else s + 1), flip(q, d))
                arrived(X.at[at], gs.at[g, s, flip(q, d), d], gr.at[g, s, flip(q, d), d])
                for to in out:
                    gather_send(to[0], to[1], flip(to[2], d), d)

    def need(g, s, a):
        while any(e[0][0] == g and e[0][1] <= s and e[0][2] // 2 in a for e in events):
            event()

    for g, s, q in first:
        for d in range(2):
            gather_send(g, s, flip(q, d), d)

    for c in spots:
        c.wait()
    places = N * blocks * subs
    slot_row = lax.broadcasted_iota(jnp.int32, (1, cap), 1)
    col = col_ref[...]
    place_row = (lax.div(col, subs) * blocks + row_ref[...]) * subs + lax.rem(col, subs)
    place_row = jnp.where(slot_row < count_ref[0], place_row, places)
    key_row = (place_row * cap + slot_row).astype(F32)
    down = lax.broadcasted_iota(jnp.int32, (cap, cap), 0)
    across = lax.broadcasted_iota(jnp.int32, (cap, cap), 1)
    keys = jnp.broadcast_to(key_row, (cap, cap))
    place_all = jnp.broadcast_to(place_row.astype(F32), (cap, cap))
    key_col = jnp.sum(jnp.where(down == across, keys, 0.0), axis=1, keepdims=True)
    place_col = jnp.sum(jnp.where(down == across, place_all, 0.0), axis=1, keepdims=True)
    rank = jnp.sum(jnp.where(keys < key_col, 1.0, 0.0), axis=1, keepdims=True)
    key_v[...] = jnp.sum(
        jnp.where(rank == across.astype(F32), key_col, 0.0), axis=0, keepdims=True
    ).astype(jnp.int32)
    spot = lax.broadcasted_iota(jnp.int32, (cap, places), 1).astype(F32)
    upto = jnp.sum(jnp.where(place_col <= spot, 1.0, 0.0), axis=0, keepdims=True)
    there = jnp.sum(jnp.where(place_col == spot, 1.0, 0.0), axis=0, keepdims=True)
    last_v[...] = jnp.where(there > 0.0, upto - 1.0, float(cap)).astype(jnp.int32)
    plan = [
        pltpu.make_async_copy(key_v, key_ref, plan_sem.at[0]),
        pltpu.make_async_copy(last_v, last_ref, plan_sem.at[1]),
    ]
    for c in plan:
        c.start()
    for c in ins[G:] + tile_copies + plan:
        c.wait()
    wt[...] = w_ref[...].T
    stage[cap] = jnp.zeros((TB, TB), BF)

    def slot_step(p, carry):
        acc, prev = carry
        key = jnp.maximum(key_ref[0, p], 0)
        slot = lax.rem(key, cap)
        place = lax.div(key, cap)
        keep = jnp.where(place == prev, 1.0, 0.0).astype(F32)
        acc = acc * keep + tiles[slot].astype(F32)
        stage[p] = acc.astype(BF)
        return acc, place

    carry = (jnp.zeros((TB, TB), F32), jnp.int32(-1))
    for k in range(4):
        carry = lax.fori_loop(cap * k // 4, cap * (k + 1) // 4, slot_step, carry)
        event()

    def place_step(o, carry):
        for r in range(blocks):
            for s in range(subs):
                tile = stage[jnp.clip(last_ref[0, (o * blocks + r) * subs + s], 0, cap)]
                at = pl.ds(pl.multiple_of((o * subs + s) * TB, TB), TB)
                dense[r * TB:(r + 1) * TB, at] = tile
                if has_t:
                    dense_t[at, r * TB:(r + 1) * TB] = tile.T
        return carry

    for k in range(2):
        lax.fori_loop(N * k // 2, N * (k + 1) // 2, place_step, 0)
        event()

    def chip_send(g, a, m, value):
        psend[g, m, :, a * hw:(a + 1) * hw] = value.astype(BF)
        at = (g, m, slice(None), lanes(a))
        send(psend.at[at], p1.at[at], p1s.at[g, a, m], p1r.at[g, a, m], partner)

    def chip_sum(g, a):
        at = slice(a * hw, (a + 1) * hw)
        for k in range(M - 1, -1, -1):
            m = lax.rem(mine + k, M)
            spot = p1.at[g, m, :, lanes(a)]
            arrived(spot, p1s.at[g, a, m], p1r.at[g, a, m])
            total = part[g, 2 * m + par, :, at] + p1[g, m, :, at].astype(F32)
            if k:
                p2s[g, k - 1, :, at] = total.astype(BF)
                spot = (g, k - 1, slice(None), lanes(a))
                send(p2s.at[spot], p2.at[spot], p2ss.at[g, a, k - 1], p2r.at[g, a, k - 1], (i, peer(k)))
            else:
                part[g, j, :, at] = total

    def rep_sum(g, a):
        at = slice(a * hw, (a + 1) * hw)
        total = part[g, j, :, at]
        for k in range(1, M):
            arrived(p2.at[g, k - 1, :, lanes(a)], p2ss.at[g, a, k - 1], p2r.at[g, a, k - 1])
            total += p2[g, k - 1, :, at].astype(F32)
        cols = slice(g * gw + a * hw, g * gw + (a + 1) * hw)
        agg[:, cols] = total.astype(BF)
        t = mm(agg[:, cols], w_ref[cols, :])
        pre[...] = t if g == 0 and a == 0 else pre[...] + t

    def block_part(g, offsets, first):
        def one(m, carry):
            total = None if first else part[g, m]
            for k in offsets:
                cols = block(node_at(k))
                t = mm(dense[block(m), cols], X[g, cols, :])
                total = t if total is None else total + t
            part[g, m] = total
            return carry

        lax.fori_loop(0, R, one, 0)

    def last_block(g, a):
        cols = block(node_at(h))
        at = slice(a * hw, (a + 1) * hw)
        need(g, h - 1, (a,))
        for k in range(M - 1, -1, -1):
            m = lax.rem(mine + k, M)
            jj = 2 * m + 1 - par
            chip_send(g, a, m, part[g, jj, :, at] + mm(dense[block(jj), cols], X[g, cols, at]))
        for m in range(M):
            jj = 2 * m + par
            part[g, jj, :, at] = part[g, jj, :, at] + mm(dense[block(jj), cols], X[g, cols, at])

    for g in range(G):
        block_part(g, [0], True)
        event()
    for s in range(h - 1):
        for g in range(G):
            need(g, s, (0, 1))
            block_part(g, [-(s + 1), s + 1], False)
    halves = [(g, a) for g in range(G) for a in range(2)]
    for k, (g, a) in enumerate(halves):
        last_block(g, a)
        if k == len(halves) - 2:
            for done in halves[:-1]:
                chip_sum(*done)
    for done in halves[-1:]:
        chip_sum(*done)
    for done in halves:
        rep_sum(*done)

    root = math.sqrt(2.0 / math.pi)
    step = 64 if rows % 64 == 0 else rows

    def act_step(b, carry):
        at = pl.ds(pl.multiple_of(b * step, step), step)
        v = pre[at, :]
        v2 = v * v
        t = jnp.tanh(root * (v + 0.044715 * (v2 * v)))
        half_up = 0.5 * (1.0 + t)
        act_ref[at, :] = (v * half_up).astype(BF)
        slope = half_up + (0.5 * v) * (1.0 - t * t) * (root * (1.0 + (3 * 0.044715) * v2))
        pg[at, :] = (c_ref[at, :].astype(F32) * slope).astype(BF)
        return carry

    lax.fori_loop(0, rows // step, act_step, 0)

    def grad_at(g, jj, a):
        return rg.at[g, jj, :, lanes(a)]

    for g in range(G):
        for a in range(2):
            cols = slice(g * gw + a * hw, g * gw + (a + 1) * hw)
            rg[g, j, :, a * hw:(a + 1) * hw] = mm(pg[...], wt[:, cols]).astype(BF)
            spot = grad_at(g, j, a)
            for k in range(1, M):
                send(spot, spot, as_.at[g, a, k], ar.at[g, a, k], (i, peer(k)))
            send(spot, spot, as_.at[g, a, 0], ar.at[g, a, 0], partner)

    def grad_forward(g, a):
        for k in range(1, M):
            spot = grad_at(g, peer(-k), a)
            arrived(spot, as_.at[g, a, k], ar.at[g, a, k])
            send(spot, spot, fs.at[g, a, k - 1], fr.at[g, a, k - 1], partner)

    def grad_ready(g, a):
        arrived(grad_at(g, j + 1 - 2 * par, a), as_.at[g, a, 0], ar.at[g, a, 0])
        for k in range(1, M):
            spot = grad_at(g, peer(-k) + 1 - 2 * par, a)
            arrived(spot, fs.at[g, a, k - 1], fr.at[g, a, k - 1])

    wr = F // R
    Z, hx = N // 2, wr // 2
    pa = min(Z, hx // 16)
    pb = Z // pa
    ph, pw = hx // pa, F // pb

    def weight_terms():
        aggt[...] = agg[...].T

        def one(k, carry):
            at = pl.ds(pl.multiple_of(k * wr, wr), wr)
            t = mm(aggt[at, :], pg[...])
            wterm[k] = t
            wsend[k] = t.astype(BF)
            return carry

        lax.fori_loop(0, R, one, 0)
        for m in range(M):
            send(wsend.at[2 * m + 1 - par], wa.at[m], was.at[m], war.at[m], partner)

    def weight_chip():
        for m in range(M):
            arrived(wa.at[m], was.at[m], war.at[m])
            wterm[2 * m + par] = wterm[2 * m + par] + wa[m].astype(F32)
        for k in range(1, M):
            to = lax.rem(mine + k, M)
            wbs[k - 1] = wterm[2 * to + par].astype(BF)
            send(wbs.at[k - 1], wb.at[k - 1], wbss.at[k - 1], wbr.at[k - 1], (i, 2 * to + par))

    across_node = (i + 1 - 2 * x, j)

    def half_rows(b):
        return pl.ds(pl.multiple_of(b * hx, hx), hx)

    def other(k):
        return lax.rem(z + k + Z, Z)

    def piece(n, base):
        return (
            pl.ds(pl.multiple_of(base + lax.div(n, pb) * ph, ph), ph),
            pl.ds(pl.multiple_of(lax.rem(n, pb) * pw, pw), pw),
        )

    def weight_rep():
        for b in (1 - x, x):
            total = wterm[j, half_rows(b), :]
            for k in range(1, M):
                if b is not x:
                    arrived(wb.at[k - 1], wbss.at[k - 1], wbr.at[k - 1])
                total += wb[k - 1, half_rows(b), :].astype(F32)
            if b is x:
                wterm[j, half_rows(b), :] = total
            else:
                wxs[...] = total.astype(BF)
                send(wxs, wx, wxsem.at[0], wxsem.at[1], across_node)

    def weight_pair():
        arrived(wx, wxsem.at[0], wxsem.at[1])
        wq[...] = (wterm[j, half_rows(x), :] + wx[...].astype(F32)).astype(BF)
        for k in range(1, Z):
            n = other(k)
            send(wq.at[piece(n, 0)], wc.at[k - 1], wcs.at[k - 1], wcr.at[k - 1], (2 * n + x, j))

    def weight_node():
        total = wq[piece(z, 0)].astype(F32)
        for k in range(1, Z):
            arrived(wc.at[k - 1], wcs.at[k - 1], wcr.at[k - 1])
            total += wc[k - 1].astype(F32)
        at = (j,) + piece(z, x * hx)
        wfull[at] = total.astype(BF)
        for k in range(1, N):
            send(wfull.at[at], wfull.at[at], wds.at[k - 1], wdr.at[k - 1], (lax.rem(i + k, N), j))

    def weight_spread():
        for k in range(1, N):
            n = lax.rem(i - k + N, N)
            at = (j,) + piece(lax.div(n, 2), lax.rem(n, 2) * hx)
            arrived(wfull.at[at], wds.at[k - 1], wdr.at[k - 1])
        spot = wfull.at[j]
        for k in range(1, M):
            send(spot, spot, wes.at[k], wer.at[k], (i, peer(k)))
        send(spot, spot, wes.at[0], wer.at[0], partner)

    def weight_forward():
        for k in range(1, M):
            spot = wfull.at[peer(-k)]
            arrived(spot, wes.at[k], wer.at[k])
            send(spot, spot, wfs.at[k - 1], wfr.at[k - 1], partner)

    def weight_end():
        arrived(wfull.at[j + 1 - 2 * par], wes.at[0], wer.at[0])
        for k in range(1, M):
            spot = wfull.at[peer(-k) + 1 - 2 * par]
            arrived(spot, wfs.at[k - 1], wfr.at[k - 1])
        wsum_ref[...] = wfull[...]

    side = [
        weight_end, weight_forward, weight_spread,
        weight_node, weight_pair, weight_rep, weight_chip,
    ]

    def term(g, o, at):
        grads = rg[g, :, :, at]
        grads = grads.reshape(R * rows, grads.shape[-1])
        if has_t:
            return mm(dense_t[block(o), :], grads)
        return lax.dot_general(
            dense[:, block(o)], grads, (((0,), (0,)), ((), ())), preferred_element_type=F32
        )

    pending = {}

    def ring_send(g, s, q, d):
        at = unit(q)
        c = rcopy(
            rsb.at[(g, s % D, d) + at], rrb.at[(g, s, d) + at],
            rs.at[g, s, q, d], rr.at[g, s, q, d], (ring_to[d], j),
        )
        c.start()
        pending[(g, s, q, d)] = c

    def cut(q):
        return slice(q % 2 * hr, (q % 2 + 1) * hr), slice(q // 2 * hw, (q // 2 + 1) * hw)

    made = set()

    def make(g, s, a):
        key = (g, s, a if s < 2 else 0)
        if key in made:
            return
        made.add(key)
        at = slice(a * hw, (a + 1) * hw) if s < 2 else slice(None)
        if s == 0 or s == h:
            tbuf[g, s % 3, 0, :, at] = term(g, node_at(h) if s == 0 else i, at)
        else:
            for d in range(2):
                tbuf[g, s % 3, d, :, at] = term(g, node_at(h - s if d == 0 else s - h), at)

    def come(g, s, q, d):
        arrived(rrb.at[(g, s, d) + unit(q)], rs.at[g, s, q, d], rr.at[g, s, q, d])
        return rrb[(g, s, d) + cut(q)].astype(F32)

    def ring_unit(g, s, u):
        make(g, s, u // 2)
        for d in range(2):
            q = flip(u, d)
            v = tbuf[(g, s % 3, d if s else 0) + cut(q)]
            if s > 1 or (s == 1 and u % 2 == 0):
                v += come(g, s - 1, q, d)
            if (g, s - D, q, d) in pending:
                pending.pop((g, s - D, q, d)).wait_send()
            rsb[(g, s % D, d) + cut(q)] = v.astype(BF)
            ring_send(g, s, q, d)

    def ring_end(g, a):
        make(g, h, a)
        for q in (2 * a, 2 * a + 1):
            v = tbuf[(g, h % 3, 0) + cut(q)]
            for d in range(2):
                v += come(g, h - 1, q, d)
            r, c = cut(q)
            fg_ref[r, g * gw + c.start:g * gw + c.stop] = v.astype(BF)

    weight_terms()
    side.pop()()
    order = []
    for g in range(G):
        for a in range(2):
            grad_forward(g, a)
            grad_ready(g, a)
            for s in range(2):
                ring_unit(g, s, 2 * a + s)
                order.append((g, s, 2 * a + s))
    n = 0
    while n < len(order):
        g, s, u = order[n]
        if s + 1 < h:
            ring_unit(g, s + 1, u)
            order.append((g, s + 1, u))
        elif all((g, s, u - u % 2 + k) in order[:n + 1] for k in range(2)):
            ring_end(g, u // 2)
        n += 1
        if n in SIDE_AT and len(side) > 1:
            side.pop()()
    while side:
        side.pop()()

    for c in sent:
        c.wait_send()
    for c in pending.values():
        c.wait_send()


def finish_kernel(scale, act_in, wsum_in, fg_in, act_out, wg_out, fg_out, wide, sems):
    copies = [
        pltpu.make_async_copy(act_in, act_out, sems.at[0]),
        pltpu.make_async_copy(fg_in, fg_out, sems.at[1]),
    ]
    for c in copies:
        c.start()
    R, wr, F = wsum_in.shape
    for k in range(R):
        at = slice(k * wr, (k + 1) * wr)
        wide[at, :] = wsum_in[k].astype(F32) * scale
        c = pltpu.make_async_copy(wide.at[at, :], wg_out.at[at, :], sems.at[2 + k])
        c.start()
        copies.append(c)
    for c in copies:
        c.wait()


def local(N, R, features, weight, cotangent, tile_values, tile_row, tile_col, tile_count):
    rows, F = features.shape
    cap = tile_values.shape[0]
    subs = rows // TB
    blocks = subs * R
    G, T, Q = 2, 4, 4
    gw, h, M = F // G, N // 2, R // 2
    D = min(h, 4)
    wr = F // R
    Z, hx = N // 2, wr // 2
    pa = min(Z, hx // 16)
    ph, pw = hx // pa, F // (Z // pa)
    places = N * blocks * subs
    has_t = N * rows * rows * R * 2 <= 8 * 1024 * 1024
    cfg = (N, R, G, D, T, cap, blocks, subs, has_t)
    dma = pltpu.SemaphoreType.DMA
    V = pltpu.VMEM
    M1 = max(M - 1, 1)
    scratch = [
        V((1, cap), jnp.int32), V((1, cap), jnp.int32),
        V((cap, TB, TB), BF), V((cap + 1, TB, TB), BF),
        V((R * rows, N * rows), BF),
        V((N * rows, R * rows) if has_t else (16, TB), BF),
        V((G, N * rows, gw), BF), V((G, R, rows, gw), F32),
        V((G, M, rows, gw), BF), V((G, M, rows, gw), BF), V((G, M1, rows, gw), BF), V((G, M1, rows, gw), BF),
        V((rows, F), BF), V((rows, F), F32), V((rows, F), BF), V((F, F), BF), V((F, F), BF), V((rows, F), BF),
        V((G, R, rows, gw), BF), V((G, D, 2, rows, gw), BF), V((G, h, 2, rows, gw), BF),
        V((G, 3, 2, rows, gw), F32), V((F, rows), BF),
        V((R, wr, F), F32), V((R, wr, F), BF), V((M, wr, F), BF),
        V((M1, wr, F), BF), V((M1, wr, F), BF),
        V((hx, F), BF), V((hx, F), BF), V((hx, F), BF), V((Z - 1, ph, pw), BF), V((R, wr, F), BF),
        V((1, cap), jnp.int32), V((1, places), jnp.int32),
        pltpu.SMEM((1, cap), jnp.int32), pltpu.SMEM((1, places), jnp.int32),
        dma((G + 2,)), dma((T,)), dma((4,)), dma((G, h, Q, 2)), dma((G, h, Q, 2)),
        dma((G, 2, M)), dma((G, 2, M)), dma((G, 2, M1)), dma((G, 2, M1)),
        dma((G, 2, M)), dma((G, 2, M)), dma((G, 2, M1)), dma((G, 2, M1)),
        dma((G, h, Q, 2)), dma((G, h, Q, 2)),
        dma((M,)), dma((M,)), dma((M,)), dma((M,)), dma((2,)),
        dma((Z - 1,)), dma((Z - 1,)), dma((N - 1,)), dma((N - 1,)),
        dma((M,)), dma((M,)), dma((M,)), dma((M,)),
    ]
    smem = pl.BlockSpec(memory_space=pltpu.SMEM)
    vmem = pl.BlockSpec(memory_space=pltpu.VMEM)
    hbm = pl.BlockSpec(memory_space=pltpu.HBM)
    act, wsum, feature_grad = pl.pallas_call(
        functools.partial(layer_kernel, cfg),
        out_shape=(
            jax.ShapeDtypeStruct((rows, F), BF),
            jax.ShapeDtypeStruct((R, wr, F), BF),
            jax.ShapeDtypeStruct((rows, F), BF),
        ),
        in_specs=[smem] + [hbm] * 6,
        out_specs=(vmem, vmem, vmem),
        scratch_shapes=scratch,
        compiler_params=pltpu.CompilerParams(
            collective_id=0, has_side_effects=True,
            vmem_limit_bytes=(48 if has_t else 63) * 1024 * 1024,
        ),
        name="layer",
    )(
        tile_count,
        *(
            pltpu.with_memory_space_constraint(v, pltpu.HBM)
            for v in (
                tile_row.reshape(1, cap), tile_col.reshape(1, cap),
                features, weight, cotangent, tile_values,
            )
        ),
    )
    scale = 1.0 / math.sqrt(rows * R * N)
    act, weight_grad, feature_grad = pl.pallas_call(
        functools.partial(finish_kernel, scale),
        out_shape=(
            jax.ShapeDtypeStruct((rows, F), BF),
            jax.ShapeDtypeStruct((F, F), F32),
            jax.ShapeDtypeStruct((rows, F), BF),
        ),
        in_specs=[vmem, vmem, vmem],
        out_specs=(hbm, hbm, hbm),
        scratch_shapes=[V((F, F), F32), dma((2 + R,))],
        compiler_params=pltpu.CompilerParams(vmem_limit_bytes=8 * 1024 * 1024),
        name="finish",
    )(act, wsum, feature_grad)
    return act, weight_grad, feature_grad


def solution(mesh):
    in_specs = (
        P(("node", "rep"), None),
        P(),
        P(("node", "rep"), None),
        P(("node", "rep"), None, None),
        P(("node", "rep")),
        P(("node", "rep")),
        P(("node", "rep")),
    )
    out_specs = (P(("node", "rep"), None), P(), P(("node", "rep"), None))
    step = functools.partial(local, mesh.shape["node"], mesh.shape["rep"])
    return jax.shard_map(step, mesh=mesh, in_specs=in_specs, out_specs=out_specs, check_vma=False)
```
